256 devices in a mesh: ctx: 64 (over x, z, core), head: 4 (over y).
Axes of the slice: x: 4, y: 4, z: 8, core: 2. Of those that a mesh axis runs over, the one named last changes fastest.
Arguments:
- layer_in: bfloat16 [16384, 2048], P(('ctx', 'head')), may hold values from -6 to 6
- in_proj: bfloat16 [2048, 8, 768], P(None, 'head'), may hold values from -0.125 to 0.125
- conv_weight: float32 [4, 8, 512], P(None, 'head'), may hold values from -2 to 2
- gate_logits: float32 [2, 16, 16384], P(None, 'head', 'ctx'), may hold values from -16 to 4
- norm_gain: float32 [128], replicated, may hold values from 0.1 to 1.9
- out_proj: bfloat16 [2048, 2048], P('head'), may hold values from -0.125 to 0.125
Outputs:
- layer_out: bfloat16 [16384, 2048], P(('ctx', 'head'))
The draws below stay inside these ranges and needn't reach their ends.
All inputs are finite; a program needn't handle non-finite values.
Results may differ from the reference program's by a relative error of at most 0.0065.
Values may be sent and summed in bfloat16 or wider, within the bound.
A program may use at most 128 MiB of HBM per device.

```python
import math
import jax
import jax.numpy as jnp
from jax import lax

D = 2048
HK = 8
VALUE_HEADS = 16
DK = 128
DV = 128
KERNEL = 4
SPAN = 64
TOK_DEV = 256
WINDOW_TOKENS = 16384


def draw_gate_logits(key, part):
    split_random_keys = jax.random.split(key, 8)
    blocks = WINDOW_TOKENS // TOK_DEV
    slow_share = 0.5
    slow_mask = (jax.random.uniform(split_random_keys[0], (VALUE_HEADS, 1)) < slow_share).astype(jnp.float32)
    fast_rate = jnp.exp(jax.random.uniform(split_random_keys[1], (VALUE_HEADS, 1), minval=math.log(1.0 / 60.0), maxval=math.log(1.0 / 20.0)))
    slow_rate = 0.15 / WINDOW_TOKENS
    base_rate = slow_mask * slow_rate + (1.0 - slow_mask) * fast_rate
    block_factor = jnp.exp(jax.random.uniform(split_random_keys[2], (VALUE_HEADS, blocks, 1), minval=math.log(0.5), maxval=math.log(2.0)))
    block_factor = jnp.broadcast_to(block_factor, (VALUE_HEADS, blocks, TOK_DEV)).reshape(VALUE_HEADS, WINDOW_TOKENS)
    token_factor = jnp.exp(jax.random.uniform(split_random_keys[3], (VALUE_HEADS, WINDOW_TOKENS), minval=math.log(0.5), maxval=math.log(2.0)))
    current_rate = base_rate * block_factor * token_factor
    surge_positions = jax.random.randint(split_random_keys[4], (VALUE_HEADS, 3, 1), 0, WINDOW_TOKENS)
    surge_flag = jnp.any(jnp.arange(WINDOW_TOKENS)[None, None, :] == surge_positions, axis=1).astype(jnp.float32)
    surge_penalty = jax.random.uniform(split_random_keys[5], (VALUE_HEADS, WINDOW_TOKENS), minval=0.2, maxval=0.35)
    current_rate = current_rate - surge_flag * jnp.log(1.0 - surge_penalty)
    decay_logit = jnp.log(jnp.expm1(current_rate))
    beta_fast = jnp.clip(jax.random.normal(split_random_keys[6], (VALUE_HEADS, WINDOW_TOKENS)), -4.0, 4.0)
    beta_value = 0.3 * DK / WINDOW_TOKENS * jnp.exp(jax.random.uniform(split_random_keys[7], (VALUE_HEADS, WINDOW_TOKENS), minval=math.log(0.5), maxval=math.log(2.0)))
    beta_slow = jnp.log(beta_value) - jnp.log1p(-beta_value)
    beta_logit = slow_mask * beta_slow + (1.0 - slow_mask) * beta_fast
    return jnp.stack([decay_logit, beta_logit]).astype(jnp.float32)


def block_levels(key, dims, shards, smallest, largest):
    level, own = 1.0, jax.random.fold_in(key, 6)
    for position, blocks in shards:
        heights = jnp.exp(jax.random.uniform(jax.random.fold_in(own, position), (blocks,), jnp.float32, smallest / len(shards), largest / len(shards)))
        level = level * jnp.repeat(heights, dims[position] // blocks).reshape([-1 if axis == position else 1 for axis in range(len(dims))])
    return level


def gaussian(stream_key, extent, scale, limit, cuts=(), kind=jnp.bfloat16):
    drawn = scale * jax.random.normal(stream_key, extent, jnp.float32)
    if cuts:
        drawn = drawn * block_levels(stream_key, extent, cuts, -0.22, 0.18)
    return jnp.clip(drawn, -limit, limit).astype(kind)


def setup_inputs(seed: int = 0) -> dict:
    keys = jax.random.split(jax.random.key(seed), 7)
    return {
        "layer_in": gaussian(keys[0], (WINDOW_TOKENS, D), 1.0, 6.0, ((0, 256),)),
        "in_proj": gaussian(keys[1], (D, HK, 2 * DK + 2 * (VALUE_HEADS // HK) * DV), D ** -0.5, 0.125, ((1, 4),)),
        "conv_weight": gaussian(keys[2], (KERNEL, HK, 2 * DK + (VALUE_HEADS // HK) * DV), 0.5, 2.0, ((1, 4),), jnp.float32),
        "gate_logits": draw_gate_logits(jax.random.fold_in(keys[6], 71), 0),
        "norm_gain": jnp.clip(1.0 + 0.18 * jax.random.normal(keys[4], (DV,), jnp.float32), 0.1, 1.9),
        "out_proj": gaussian(keys[5], (VALUE_HEADS * DV, D), (VALUE_HEADS * DV) ** -0.5, 0.125, ((0, 4),)),
    }


EPSILON = 1e-06
HIGHEST_PREC = lax.Precision.HIGHEST

def product(pattern, first, second):
    return jnp.einsum(pattern, first, second, precision=HIGHEST_PREC)

def causal_conv(padded, weight, length):
    taps_count = weight.shape[0]
    running = padded[0:length] * weight[0]
    for offset in range(1, taps_count):
        running = running + padded[offset:offset + length] * weight[offset]
    return running

def l2_normed(values):
    return values * lax.rsqrt(lax.optimization_barrier(jnp.sum(values * values, axis=-1, keepdims=True)) + EPSILON)

def unit_inverse(lower_mat):
    size_now = lower_mat.shape[-1]
    levels = max((size_now - 1).bit_length(), 1)
    identity = jnp.eye(size_now, dtype=lower_mat.dtype)
    power = -lower_mat
    result = identity + power
    for level_index in range(1, levels):
        power = product('...ij,...jk->...ik', power, power)
        result = product('...ij,...jk->...ik', result, identity + power)
    return result

def span_terms(queries, key_rows, values, log_decay, beta_gate):
    cum_decay = jnp.cumsum(log_decay, axis=-1)
    row_ids = jnp.arange(log_decay.shape[-1])
    strict_below = row_ids[:, None] > row_ids[None, :]
    on_or_below = row_ids[:, None] >= row_ids[None, :]
    log_gap = cum_decay[..., :, None] - cum_decay[..., None, :]
    decay_mat = jnp.where(on_or_below, jnp.exp(jnp.where(on_or_below, log_gap, 0.0)), 0.0)
    key_gram = product('...id,...jd->...ij', key_rows, key_rows)
    lower_mat = jnp.where(strict_below, beta_gate[..., :, None] * key_gram * decay_mat, 0.0)
    solver = unit_inverse(lower_mat)
    scaled_k = key_rows * (beta_gate * jnp.exp(cum_decay))[..., None]
    scaled_v = values * beta_gate[..., None]
    w_rows = product('...ij,...jd->...id', solver, scaled_k)
    u_rows = product('...ij,...jd->...id', solver, scaled_v)
    qk_mat = product('...id,...jd->...ij', queries, key_rows) * decay_mat
    q_dec = queries * jnp.exp(cum_decay)[..., None]
    k_dec = key_rows * jnp.exp(cum_decay[..., -1:] - cum_decay)[..., None]
    span_decay = jnp.exp(cum_decay[..., -1])
    return (w_rows, u_rows, qk_mat, q_dec, k_dec, span_decay)

def reference(layer_in, in_proj, conv_weight, gate_logits, norm_gain, out_proj):
    group_ratio = VALUE_HEADS // HK
    conv_width = 2 * DK + group_ratio * DV
    group_width = conv_width + group_ratio * DV
    projected = jnp.dot(layer_in, in_proj.reshape(D, HK * group_width), preferred_element_type=jnp.float32).astype(jnp.bfloat16)
    projected = projected.reshape(WINDOW_TOKENS, HK, group_width)
    conv_in = projected[:, :, :conv_width].astype(jnp.float32)
    padded = jnp.concatenate([jnp.zeros((KERNEL - 1, HK, conv_width), jnp.float32), conv_in], axis=0)
    conv_out = jax.nn.silu(causal_conv(padded, conv_weight, WINDOW_TOKENS))
    queries = l2_normed(conv_out[:, :, :DK]) * DK ** (-0.5)
    key_rows = l2_normed(conv_out[:, :, DK:2 * DK])
    values = conv_out[:, :, 2 * DK:].reshape(WINDOW_TOKENS, VALUE_HEADS, DV)
    gate_z = projected[:, :, conv_width:].reshape(WINDOW_TOKENS, VALUE_HEADS, DV).astype(jnp.float32)
    queries = jnp.repeat(queries, group_ratio, axis=1)
    key_rows = jnp.repeat(key_rows, group_ratio, axis=1)
    spans = WINDOW_TOKENS // SPAN

    def by_span(array_in):
        return array_in.reshape(spans, SPAN, VALUE_HEADS, -1).transpose(0, 2, 1, 3)
    log_decay = (-jax.nn.softplus(gate_logits[0])).reshape(VALUE_HEADS, spans, SPAN).transpose(1, 0, 2)
    beta_gate = jax.nn.sigmoid(gate_logits[1]).reshape(VALUE_HEADS, spans, SPAN).transpose(1, 0, 2)

    def advance(carried, pieces):
        w_rows, u_rows, qk_mat, q_dec, k_dec, span_decay = span_terms(*pieces)
        fresh_values = u_rows - product('hcd,hde->hce', w_rows, carried)
        result = product('hcd,hde->hce', q_dec, carried) + product('hij,hje->hie', qk_mat, fresh_values)
        carried = span_decay[:, None, None] * carried + product('hcd,hce->hde', k_dec, fresh_values)
        return (carried, result)
    start_state = jnp.zeros((VALUE_HEADS, DK, DV), jnp.float32)
    final_state, outputs = lax.scan(advance, start_state, (by_span(queries), by_span(key_rows), by_span(values), log_decay, beta_gate))
    attended = outputs.transpose(0, 2, 1, 3).reshape(WINDOW_TOKENS, VALUE_HEADS, DV)
    mean_square = lax.optimization_barrier(jnp.mean(attended * attended, axis=-1, keepdims=True))
    normed = (attended * lax.rsqrt(mean_square + EPSILON) * norm_gain * jax.nn.silu(gate_z)).astype(jnp.bfloat16)
    normed = normed.reshape(WINDOW_TOKENS, VALUE_HEADS * DV)
    return jnp.dot(normed, out_proj, preferred_element_type=jnp.float32).astype(jnp.bfloat16)
```

```python
import functools

import jax
import jax.numpy as jnp
from jax import lax
from jax.experimental import pallas as pl
from jax.experimental.pallas import tpu as pltpu
from jax.sharding import PartitionSpec as P

NX, NZ, NC = 4, 8, 2
DK = 128
GROUP = 768
TOK = 256
HALO = 16
EPS = 1e-06
MESH = pl.DeviceIdType.MESH
F32, BF16 = jnp.float32, jnp.bfloat16


def dot(a, b):
    return lax.dot_general(a, b, (((1,), (0,)), ((), ())), preferred_element_type=F32)


def dot_nt(a, b):
    return lax.dot_general(a, b, (((1,), (1,)), ((), ())), preferred_element_type=F32)


def split(a):
    hi = a.astype(BF16)
    return hi, (a - hi.astype(F32)).astype(BF16)


def dot3(a, b, op=dot):
    ah, al = split(a)
    bh, bl = split(b)
    return op(ah, bh) + (op(al, bh) + op(ah, bl))


def dot2(a, b, op=dot):
    ah, al = split(a)
    return op(ah, b) + op(al, b)


def iota(shape, dim):
    return lax.broadcasted_iota(jnp.int32, shape, dim)


def silu(a):
    return a * jax.nn.sigmoid(a)


def log1p(u):
    series = u * (1.0 - u * (0.5 - u * (1.0 / 3.0 - u * 0.25)))
    return jnp.where(u < 1.0 / 64.0, series, jnp.log(1.0 + u))


def kernel(
    ny,
    x_ref,
    w_ref,
    cw_ref,
    gate_ref,
    gain_ref,
    wo_ref,
    out_ref,
    xg,
    w3,
    w2,
    tmp,
    pj,
    wo,
    qs,
    ks,
    dec,
    wus,
    gs,
    os_,
    nrm,
    pair,
    comb,
    hbuf,
    st,
    xbuf,
    sin,
    obuf,
    sbuf,
    rst,
    rbuf,
    w_sem,
    loc_sem,
    ag_send,
    ag_recv,
    halo_send,
    halo_recv,
    l0_send,
    l0_recv,
    p1_send,
    p1_recv,
    p2_send,
    p2_recv,
    p3_send,
    p3_recv,
    rs_send,
    rs_recv,
):
    c = lax.axis_index("ctx")
    y = lax.axis_index("head")
    nctx = NX * NZ * NC
    k = lax.rem(c, NC)
    z = lax.rem(c // NC, NZ)
    x = c // (NC * NZ)
    handler = k == z // (NZ // NC)
    p = lax.rem(z, 2)
    zs = z + 1 - 2 * p

    def at(xx, zz, kk):
        return ((xx * NZ + zz) * NC + kk, y)

    rows_w = w3.shape[0] // 4
    w_copies = []
    for i in range(4):
        part = pl.ds(i * rows_w, rows_w)
        w_copies.append(pltpu.make_async_copy(w_ref.at[part], w3.at[part], w_sem.at[i]))
        w_copies[-1].start()
    own_rows = pl.ds(pl.multiple_of(HALO + 64 * y, 16), 64)
    own_x = pltpu.make_async_copy(x_ref, xg.at[own_rows], loc_sem.at[0])
    own_x.start()

    barrier = pltpu.get_barrier_semaphore()

    def hello(target):
        pl.semaphore_signal(barrier, inc=1, device_id=target, device_id_type=MESH)

    for o in range(1, ny):
        hello((c, lax.rem(y + o, ny)))

    @pl.when(c > 0)
    def _():
        hello((c - 1, ny - 1))

    for o in range(1, NZ * NC):
        hello((x * (NZ * NC) + lax.rem(z * NC + k + o, NZ * NC), y))
    for o in range(NX - 1):

        @pl.when(handler & (x > o))
        def _():
            hello(at(o, z, k))
            hello(at(o, zs, k))

    halo_out = jnp.where((y == ny - 1) & (c < nctx - 1), ny, 0)
    later = jnp.where(handler, 2 * (NX - 1 - x), 0)
    pl.semaphore_wait(barrier, ny - 1 + NZ * NC - 1 + halo_out + later)

    def ag_copy(o):
        return pltpu.make_async_remote_copy(
            src_ref=x_ref,
            dst_ref=xg.at[own_rows],
            send_sem=ag_send.at[o - 1],
            recv_sem=ag_recv.at[o - 1],
            device_id=(c, lax.rem(y + o, ny)),
            device_id_type=MESH,
        )

    def halo_copy(yy):
        return pltpu.make_async_remote_copy(
            src_ref=x_ref.at[pl.ds(64 - HALO, HALO)],
            dst_ref=xg.at[pl.ds(0, HALO)],
            send_sem=halo_send.at[yy],
            recv_sem=halo_recv.at[0],
            device_id=(c + 1, yy),
            device_id_type=MESH,
        )

    for o in (2, 1, 3):
        if o < ny:
            ag_copy(o).start()

    @pl.when((y == ny - 1) & (c < nctx - 1))
    def _():
        for yy in range(ny):
            halo_copy(yy).start()

    wo_copy = pltpu.make_async_copy(wo_ref, wo, loc_sem.at[1])
    wo_copy.start()

    w2d = w3.reshape(2 * w3.shape[0], GROUP)
    for i in range(4):
        w_copies[i].wait()

        @pl.loop(i * rows_w // 64, (i + 1) * rows_w // 64)
        def _(s):
            r = pl.ds(pl.multiple_of(s * 64, 64), 64)
            r2 = pl.ds(pl.multiple_of(s * 128, 128), 128)
            for b in range(0, GROUP, 128):
                tmp[b : b + 128, :] = w2d[r2, b : b + 128].astype(F32)
            for g in range(2):
                for b in range(0, GROUP, 128):
                    piece = tmp[pl.ds(b + g, 64, stride=2), :]
                    w2[r, g * GROUP + b : g * GROUP + b + 128] = piece.astype(BF16)

    alog = gate_ref[0]
    log_decay = -(jnp.maximum(alog, 0.0) + log1p(jnp.exp(-jnp.abs(alog))))
    beta_row = jax.nn.sigmoid(gate_ref[1])
    both = jnp.concatenate([log_decay, beta_row], axis=0)
    upper = (iota((TOK, TOK), 0) <= iota((TOK, TOK), 1)).astype(F32)
    crow = jnp.dot(both, upper, precision=lax.Precision.HIGHEST, preferred_element_type=F32)
    cols = jnp.concatenate([crow[:4], beta_row], axis=0).T

    own_x.wait()
    for o in (1, 3, 2):
        if o < ny:
            ag_copy(o).wait_recv()

    @pl.when(c > 0)
    def _():
        halo_copy(0).wait_recv()

    @pl.when(c == 0)
    def _():
        xg[0:HALO, :] = jnp.zeros((HALO, xg.shape[1]), BF16)

    for b in range(0, 2 * GROUP, 512):
        pj[:, b : b + 512] = dot(xg[...], w2[:, b : b + 512]).astype(BF16).astype(F32)

    def conv(g, b):
        col = g * GROUP + b * 128
        total = None
        for i in range(4):
            w = cw_ref[i, pl.ds(g, 1), b * 128 : b * 128 + 128]
            term = pj[HALO - 3 + i : HALO - 3 + i + TOK, col : col + 128] * w
            total = term if total is None else total + term
        return silu(total)

    def unit(u):
        return u * lax.rsqrt(jnp.sum(u * u, axis=-1, keepdims=True) + EPS)

    below = iota((TOK, TOK), 0) > iota((TOK, TOK), 1)
    on_or_below = iota((TOK, TOK), 0) >= iota((TOK, TOK), 1)
    i128, j128 = iota((128, 128), 0), iota((128, 128), 1)
    eye = (i128 == j128).astype(F32)

    blocks, lows, rhs = [], [], []
    for g in range(2):
        qs[g] = unit(conv(g, 0)) * (DK**-0.5)
        key = unit(conv(g, 1))
        ks[g] = key
        gram = dot3(key, key, dot_nt)
        for r in range(2):
            h = 2 * g + r
            value = conv(g, 2 + r)
            ccol, bcol = cols[:, h : h + 1], cols[:, 4 + h : 5 + h]
            gap = ccol - crow[h : h + 1, :]
            decay = jnp.where(on_or_below, jnp.exp(jnp.where(on_or_below, gap, 0.0)), 0.0)
            dec[h] = decay
            low = jnp.where(below, bcol * gram * decay, 0.0)
            blocks.append(low[:128, :128])
            blocks.append(low[128:, 128:])
            lows.append(low[128:, :128])
            rhs.append(jnp.concatenate([key * (bcol * jnp.exp(ccol)), value * bcol], axis=1))

    def same(size):
        return (i128 // size) == (j128 // size)

    power = [jnp.where(same(8), -a, 0.0) for a in blocks]
    inv = [eye + a for a in power]
    for _ in range(2):
        power = [dot3(a, a) for a in power]
        inv = [b + dot3(b, a) for a, b in zip(power, inv)]
    for size in (8, 16, 32, 64):
        off = same(2 * size) & jnp.logical_not(same(size))
        mid = [dot3(jnp.where(off, a, 0.0), b) for a, b in zip(blocks, inv)]
        inv = [b - dot3(b, a) for a, b in zip(mid, inv)]

    first = [dot3(inv[2 * h], rhs[h][:128]) for h in range(4)]
    second = [rhs[h][128:] - dot3(lows[h], first[h]) for h in range(4)]
    second = [dot3(inv[2 * h + 1], second[h]) for h in range(4)]
    for h in range(4):
        wu = jnp.concatenate([first[h], second[h]], axis=0)
        wus[h] = wu
        last = crow[h : h + 1, TOK - 1 : TOK]
        k_dec = ks[h // 2] * jnp.exp(last - cols[:, h : h + 1])
        total = dot3(wu.T, k_dec)
        pair[k, h, 0:128, :] = (eye * (1.0 - jnp.exp(last)) + total[:128]).astype(BF16)
        pair[k, h, 128:256, :] = total[128:].astype(BF16)

    def l0_copy(h):
        return pltpu.make_async_remote_copy(
            src_ref=pair.at[k, h],
            dst_ref=pair.at[k, h],
            send_sem=l0_send.at[h],
            recv_sem=l0_recv.at[h],
            device_id=(c + 1 - 2 * k, y),
            device_id_type=MESH,
        )

    l0_copy(0).start()
    l0_copy(1).start()

    @pl.when(k == 0)
    def _():
        l0_copy(2).start()
        l0_copy(3).start()

    l0_copy(0).wait_recv()
    l0_copy(1).wait_recv()

    @pl.when(k == 1)
    def _():
        l0_copy(2).wait_recv()
        l0_copy(3).wait_recv()

    for j in range(2):
        h = 2 * k + j
        one, two = pair[0, h], pair[1, h]
        new = one.astype(F32) + two.astype(F32) - dot(one, two[:128])
        new = new.astype(BF16)
        comb[j, 0:64] = new[128:192]
        comb[j, 64:192] = new[0:128]
        comb[j, 192:256] = new[192:256]

    def p1_args(n):
        j, half = n // 2, n % 2
        return comb.at[j, pl.ds(64 * half, 192)], hbuf.at[z], 4 * k + n

    def p1_remote(n):
        src, dst, zz = p1_args(n)
        return pltpu.make_async_remote_copy(
            src_ref=src,
            dst_ref=dst,
            send_sem=p1_send.at[n],
            recv_sem=p1_recv.at[0],
            device_id=at(x, zz, k),
            device_id_type=MESH,
        )

    for n in range(4):

        @pl.when(z != 4 * k + n)
        def _():
            p1_remote(n).start()

        @pl.when(z == 4 * k + n)
        def _():
            src, dst, _ = p1_args(n)
            pltpu.make_async_copy(src, dst, p1_recv.at[0]).start()

    for g in range(2):
        qk = dot3(qs[g], ks[g], dot_nt)
        for r in range(2):
            h = 2 * g + r
            both_parts = dot3(qk * dec[h], wus[h])
            gs[h] = qs[g] * jnp.exp(cols[:, h : h + 1]) - both_parts[:, :128]
            os_[h] = both_parts[:, 128:]

    def p2_copy(xx, sibling):
        if sibling:
            src = st.at[pl.ds(64, 64)]
            dst = xbuf.at[x, pl.ds(pl.multiple_of(128 * p, 64), 64)]
            target = at(xx, zs, k)
        else:
            rows = pl.ds(pl.multiple_of(64 * p, 64), 128)
            src, dst, target = st.at[rows], xbuf.at[x, rows], at(xx, z, k)
        return pltpu.make_async_remote_copy(
            src_ref=src,
            dst_ref=dst,
            send_sem=p2_send.at[2 * xx + sibling],
            recv_sem=p2_recv.at[x],
            device_id=target,
            device_id_type=MESH,
        )

    def p3_remote(i, kk):
        return pltpu.make_async_remote_copy(
            src_ref=obuf.at[i],
            dst_ref=sbuf.at[z // 2, pl.ds(pl.multiple_of(64 * p, 64), 64)],
            send_sem=p3_send.at[NC * i + kk],
            recv_sem=p3_recv.at[0],
            device_id=at(x, i, kk),
            device_id_type=MESH,
        )

    @pl.when(handler)
    def _():
        pltpu.make_async_copy(hbuf, hbuf, p1_recv.at[0]).wait()
        r_rows = pl.ds(pl.multiple_of(64 * (1 - p), 64), 128)
        s_rows = pl.ds(pl.multiple_of(128 * p, 64), 64)

        def leaf(i):
            return hbuf[i, r_rows], hbuf[i, s_rows]

        def leaf_stack(i):
            r, s = leaf(i)
            return jnp.concatenate([r, s], axis=0)

        twos = []
        for i in range(0, 8, 2):
            a, b = leaf_stack(i), leaf_stack(i + 1)
            twos.append(a.astype(F32) + b.astype(F32) - dot(a, b[:128]))
        fours = [a + b - dot3(a, b[:128]) for a, b in zip(twos[::2], twos[1::2])]
        row = fours[0] + fours[1] - dot3(fours[0], fours[1][:128])
        st[s_rows, :] = row[128:].astype(BF16)

        @pl.when(p == 0)
        def _():
            st[64:128, :] = row[0:64].astype(BF16)

        @pl.when(p == 1)
        def _():
            st[64:128, :] = row[64:128].astype(BF16)

        for xx in range(1, NX):

            @pl.when(x < xx)
            def _():
                p2_copy(xx, 0).start()
                p2_copy(xx, 1).start()

        sin[...] = jnp.zeros((64, 128), F32)
        for o in range(NX - 1):

            @pl.when(x > o)
            def _():
                pltpu.make_async_copy(xbuf.at[o], xbuf.at[o], p2_recv.at[o]).wait()
                now = sin[...]
                sin[...] = now - dot2(now, xbuf[o, r_rows]) + xbuf[o, s_rows].astype(F32)

        def step(state, i):
            r, s = leaf(i)
            return state - dot2(state, r) + s.astype(F32)

        def jump(state, node):
            return state - dot3(state, node[:128]) + node[128:]

        s0 = sin[...]
        s4 = jump(s0, fours[0])
        s2 = jump(s0, twos[0])
        s6 = jump(s4, twos[2])
        states = [s0, step(s0, 0), s2, step(s2, 2), s4, step(s4, 4), s6, step(s6, 6)]
        for i in range(NZ):
            obuf[i] = states[i].astype(BF16)
        for i in range(NZ):
            for kk in range(NC):
                me = (z == i) & (k == kk)

                @pl.when(jnp.logical_not(me))
                def _():
                    p3_remote(i, kk).start()

                @pl.when(me)
                def _():
                    pltpu.make_async_copy(
                        obuf.at[i],
                        sbuf.at[z // 2, pl.ds(pl.multiple_of(64 * p, 64), 64)],
                        p3_recv.at[0],
                    ).start()

    pltpu.make_async_copy(sbuf, sbuf, p3_recv.at[0]).wait()

    for h in range(4):
        g, r = h // 2, h % 2
        state = sbuf[h]
        moved = state.astype(F32) - dot(state, pair[0, h, 0:128]) + pair[0, h, 128:256].astype(F32)
        state = jnp.where(k == 1, moved, state.astype(F32))
        o = os_[h] + dot3(gs[h], state, dot_nt)
        col = g * GROUP + 512 + r * 128
        gate = silu(pj[HALO : HALO + TOK, col : col + 128])
        mean = jnp.mean(o * o, axis=-1, keepdims=True)
        nrm[:, h * 128 : h * 128 + 128] = (
            o * lax.rsqrt(mean + EPS) * gain_ref[...] * gate
        ).astype(BF16)

    wo_copy.wait()

    def part(o):
        rows = pl.ds(pl.multiple_of(64 * lax.rem(y + o, ny), 64), 64)
        return dot(nrm[rows, :], wo[...])

    def rs_copy(o):
        return pltpu.make_async_remote_copy(
            src_ref=rst.at[o - 1],
            dst_ref=rbuf.at[o - 1],
            send_sem=rs_send.at[o - 1],
            recv_sem=rs_recv.at[o - 1],
            device_id=(c, lax.rem(y + o, ny)),
            device_id_type=MESH,
        )

    for o in (2, 1, 3):
        if o < ny:
            rst[o - 1] = part(o).astype(BF16)
            rs_copy(o).start()
    acc = part(0)
    for o in (1, 3, 2):
        if o < ny:
            rs_copy(o).wait_recv()
            acc = acc + rbuf[o - 1].astype(F32)
    out_ref[...] = acc.astype(BF16)

    for o in range(1, ny):
        ag_copy(o).wait_send()
        rs_copy(o).wait_send()

    @pl.when((y == ny - 1) & (c < nctx - 1))
    def _():
        for yy in range(ny):
            halo_copy(yy).wait_send()

    l0_copy(0).wait_send()
    l0_copy(1).wait_send()

    @pl.when(k == 0)
    def _():
        l0_copy(2).wait_send()
        l0_copy(3).wait_send()

    for n in range(4):

        @pl.when(z != 4 * k + n)
        def _():
            p1_remote(n).wait_send()

    @pl.when(handler)
    def _():
        for xx in range(1, NX):

            @pl.when(x < xx)
            def _():
                p2_copy(xx, 0).wait_send()
                p2_copy(xx, 1).wait_send()

        for i in range(NZ):
            for kk in range(NC):

                @pl.when(jnp.logical_not((z == i) & (k == kk)))
                def _():
                    p3_remote(i, kk).wait_send()


def local(ny, layer_in, in_proj, conv_weight, gate_logits, norm_gain, out_proj):
    rows, width = layer_in.shape
    vmem = pl.BlockSpec(memory_space=pltpu.VMEM)
    hbm = pl.BlockSpec(memory_space=pl.ANY)
    dma = pltpu.SemaphoreType.DMA
    return pl.pallas_call(
        functools.partial(kernel, ny),
        out_shape=jax.ShapeDtypeStruct((rows, width), BF16),
        in_specs=[hbm, hbm, vmem, vmem, vmem, hbm],
        out_specs=vmem,
        scratch_shapes=[
            pltpu.VMEM((HALO + TOK, width), BF16),
            pltpu.VMEM(in_proj.shape, BF16),
            pltpu.VMEM((width, 2 * GROUP), BF16),
            pltpu.VMEM((GROUP, 128), F32),
            pltpu.VMEM((HALO + TOK, 2 * GROUP), F32),
            pltpu.VMEM(out_proj.shape, BF16),
            pltpu.VMEM((2, TOK, 128), F32),
            pltpu.VMEM((2, TOK, 128), F32),
            pltpu.VMEM((4, TOK, TOK), F32),
            pltpu.VMEM((4, TOK, 256), F32),
            pltpu.VMEM((4, TOK, 128), F32),
            pltpu.VMEM((4, TOK, 128), F32),
            pltpu.VMEM((TOK, 512), BF16),
            pltpu.VMEM((2, 4, 256, 128), BF16),
            pltpu.VMEM((2, 256, 128), BF16),
            pltpu.VMEM((NZ, 192, 128), BF16),
            pltpu.VMEM((192, 128), BF16),
            pltpu.VMEM((NX, 192, 128), BF16),
            pltpu.VMEM((64, 128), F32),
            pltpu.VMEM((NZ, 64, 128), BF16),
            pltpu.VMEM((4, 128, 128), BF16),
            pltpu.VMEM((3, 64, width), BF16),
            pltpu.VMEM((3, 64, width), BF16),
            dma((4,)),
            dma((2,)),
            dma((3,)),
            dma((3,)),
            dma((4,)),
            dma((1,)),
            dma((4,)),
            dma((4,)),
            dma((4,)),
            dma((1,)),
            dma((2 * NX,)),
            dma((NX,)),
            dma((NZ * NC,)),
            dma((1,)),
            dma((3,)),
            dma((3,)),
        ],
        compiler_params=pltpu.CompilerParams(
            collective_id=0, has_side_effects=True, vmem_limit_bytes=56 << 20
        ),
    )(layer_in, in_proj, conv_weight, gate_logits, norm_gain.reshape(1, -1), out_proj)


def solution(mesh):
    in_specs = (
        P(("ctx", "head"), None),
        P(None, "head", None),
        P(None, "head", None),
        P(None, "head", "ctx"),
        P(),
        P("head", None),
    )
    out_specs = P(("ctx", "head"), None)
    return jax.shard_map(
        functools.partial(local, mesh.shape["head"]),
        mesh=mesh,
        in_specs=in_specs,
        out_specs=out_specs,
        check_vma=False,
    )
```

```python
import functools

import jax
import jax.numpy as jnp
from jax import lax
from jax.experimental import pallas as pl
from jax.experimental.pallas import tpu as pltpu
from jax.sharding import PartitionSpec as P

NX, NZ, NC = 4, 8, 2
DK = 128
GROUP = 768
TOK = 256
HALO = 16
EPS = 1e-06
MESH = pl.DeviceIdType.MESH
F32, BF16 = jnp.float32, jnp.bfloat16


def dot(a, b):
    return lax.dot_general(a, b, (((1,), (0,)), ((), ())), preferred_element_type=F32)


def dot_nt(a, b):
    return lax.dot_general(a, b, (((1,), (1,)), ((), ())), preferred_element_type=F32)


def split(a):
    hi = a.astype(BF16)
    return hi, (a - hi.astype(F32)).astype(BF16)


def dot3(a, b, op=dot):
    ah, al = split(a)
    bh, bl = split(b)
    return op(ah, bh) + (op(al, bh) + op(ah, bl))


def dot2(a, b, op=dot):
    ah, al = split(a)
    return op(ah, b) + op(al, b)


def iota(shape, dim):
    return lax.broadcasted_iota(jnp.int32, shape, dim)


def silu(a):
    return a * jax.nn.sigmoid(a)


def log1p(u):
    series = u * (1.0 - u * (0.5 - u * (1.0 / 3.0 - u * 0.25)))
    return jnp.where(u < 1.0 / 64.0, series, jnp.log(1.0 + u))


def kernel(
    ny,
    x_ref,
    w_ref,
    cw_ref,
    gate_ref,
    gain_ref,
    wo_ref,
    out_ref,
    xg,
    w3,
    w2,
    tmp,
    pj,
    wo,
    qs,
    ks,
    dec,
    wus,
    gs,
    os_,
    nrm,
    pair,
    comb,
    hbuf,
    st,
    xbuf,
    sin,
    obuf,
    sbuf,
    ahead_n,
    ahead_s,
    rst,
    rbuf,
    round_sem,
    w_sem,
    loc_sem,
    ag_send,
    ag_recv,
    halo_send,
    halo_recv,
    l0_send,
    l0_recv,
    p1_send,
    p1_recv,
    p2_send,
    p2_recv,
    p3_send,
    p3_recv,
    rs_send,
    rs_recv,
):
    c = lax.axis_index("ctx")
    y = lax.axis_index("head")
    nctx = NX * NZ * NC
    k = lax.rem(c, NC)
    z = lax.rem(c // NC, NZ)
    x = c // (NC * NZ)
    handler = k == z // (NZ // NC)
    p = lax.rem(z, 2)
    zs = z + 1 - 2 * p

    def at(xx, zz, kk):
        return ((xx * NZ + zz) * NC + kk, y)

    xg[0:HALO, :] = jnp.zeros((HALO, xg.shape[1]), BF16)

    rows_w = w3.shape[0] // 4
    w_copies = []
    for i in range(4):
        part = pl.ds(i * rows_w, rows_w)
        w_copies.append(pltpu.make_async_copy(w_ref.at[part], w3.at[part], w_sem.at[i]))
        w_copies[-1].start()
    own_rows = pl.ds(pl.multiple_of(HALO + 64 * y, 16), 64)
    own_x = pltpu.make_async_copy(x_ref, xg.at[own_rows], loc_sem.at[0])
    own_x.start()

    barrier = pltpu.get_barrier_semaphore()

    def hello(target):
        pl.semaphore_signal(barrier, inc=1, device_id=target, device_id_type=MESH)

    up, down = lax.rem(y + 1, ny), lax.rem(y + ny - 1, ny)
    hello((c, up))
    hello((c, down))
    hello((lax.rem(c + 1, nctx), y))
    hello((lax.rem(c + nctx - 1, nctx), y))

    @pl.when(c > 0)
    def _():
        hello((c - 1, ny - 1))

    halo_out = jnp.where((y == ny - 1) & (c < nctx - 1), ny, 0)
    pl.semaphore_wait(barrier, 4 + halo_out)

    def wider(n):
        for step in (2**n, nctx - 2**n):
            pl.semaphore_signal(
                round_sem.at[n],
                inc=1,
                device_id=(lax.rem(c + step, nctx), y),
                device_id_type=MESH,
            )
        pl.semaphore_wait(round_sem.at[n], 2)

    def block_rows(yy, half):
        return pl.ds(pl.multiple_of(HALO + 64 * yy + 32 * half, 16), 32)

    def ag_copy(way, half, hop):
        owner = y if hop == 0 else (down if way == 0 else up)
        src = x_ref.at[pl.ds(32 * half, 32)] if hop == 0 else xg.at[block_rows(owner, half)]
        n = 3 * way + (2 if hop else (half if way == 0 else 1 - half))
        return pltpu.make_async_remote_copy(
            src_ref=src,
            dst_ref=xg.at[block_rows(owner, half)],
            send_sem=ag_send.at[n],
            recv_sem=ag_recv.at[n],
            device_id=(c, up if way == 0 else down),
            device_id_type=MESH,
        )

    def halo_copy(yy):
        return pltpu.make_async_remote_copy(
            src_ref=x_ref.at[pl.ds(64 - 8, 8)],
            dst_ref=xg.at[pl.ds(HALO - 8, 8)],
            send_sem=halo_send.at[yy],
            recv_sem=halo_recv.at[0],
            device_id=(c + 1, yy),
            device_id_type=MESH,
        )

    ag_copy(0, 0, 0).start()
    ag_copy(1, 1, 0).start()
    ag_copy(0, 1, 0).start()
    ag_copy(1, 0, 0).start()

    @pl.when((y == ny - 1) & (c < nctx - 1))
    def _():
        for yy in range(ny):
            halo_copy(yy).start()

    wo_copy = pltpu.make_async_copy(wo_ref, wo, loc_sem.at[1])
    wo_copy.start()

    w2d = w3.reshape(2 * w3.shape[0], GROUP)
    for i in range(4):
        w_copies[i].wait()

        @pl.loop(i * rows_w // 64, (i + 1) * rows_w // 64)
        def _(s):
            r = pl.ds(pl.multiple_of(s * 64, 64), 64)
            r2 = pl.ds(pl.multiple_of(s * 128, 128), 128)
            for b in range(0, GROUP, 128):
                tmp[b : b + 128, :] = w2d[r2, b : b + 128].astype(F32)
            for g in range(2):
                for b in range(0, GROUP, 128):
                    piece = tmp[pl.ds(b + g, 64, stride=2), :]
                    w2[r, g * GROUP + b : g * GROUP + b + 128] = piece.astype(BF16)

        wider(i)
        if i == 1:
            ag_copy(0, 0, 0).wait_recv()
            ag_copy(0, 0, 1).start()
            ag_copy(1, 1, 0).wait_recv()
            ag_copy(1, 1, 1).start()

    wider(4)

    alog = gate_ref[0]
    log_decay = -(jnp.maximum(alog, 0.0) + log1p(jnp.exp(-jnp.abs(alog))))
    beta_row = jax.nn.sigmoid(gate_ref[1])
    both = jnp.concatenate([log_decay, beta_row], axis=0)
    upper = (iota((TOK, TOK), 0) <= iota((TOK, TOK), 1)).astype(F32)
    crow = jnp.dot(both, upper, precision=lax.Precision.HIGHEST, preferred_element_type=F32)
    cols = jnp.concatenate([crow[:4], beta_row], axis=0).T

    own_x.wait()
    ag_copy(0, 1, 0).wait_recv()
    ag_copy(1, 0, 0).wait_recv()

    @pl.when(c > 0)
    def _():
        halo_copy(0).wait_recv()

    ag_copy(0, 0, 1).wait_recv()
    ag_copy(1, 1, 1).wait_recv()

    for b in range(0, 2 * GROUP, 512):
        pj[:, b : b + 512] = dot(xg[...], w2[:, b : b + 512]).astype(BF16).astype(F32)

    def conv(g, b):
        col = g * GROUP + b * 128
        total = None
        for i in range(4):
            w = cw_ref[i, pl.ds(g, 1), b * 128 : b * 128 + 128]
            term = pj[HALO - 3 + i : HALO - 3 + i + TOK, col : col + 128] * w
            total = term if total is None else total + term
        return silu(total)

    def unit(u):
        return u * lax.rsqrt(jnp.sum(u * u, axis=-1, keepdims=True) + EPS)

    below = iota((TOK, TOK), 0) > iota((TOK, TOK), 1)
    on_or_below = iota((TOK, TOK), 0) >= iota((TOK, TOK), 1)
    i128, j128 = iota((128, 128), 0), iota((128, 128), 1)
    eye = (i128 == j128).astype(F32)

    blocks, lows, rhs = [], [], []
    for g in range(2):
        qs[g] = unit(conv(g, 0)) * (DK**-0.5)
        key = unit(conv(g, 1))
        ks[g] = key
        gram = dot3(key, key, dot_nt)
        for r in range(2):
            h = 2 * g + r
            value = conv(g, 2 + r)
            ccol, bcol = cols[:, h : h + 1], cols[:, 4 + h : 5 + h]
            gap = ccol - crow[h : h + 1, :]
            decay = jnp.where(on_or_below, jnp.exp(jnp.where(on_or_below, gap, 0.0)), 0.0)
            dec[h] = decay
            low = jnp.where(below, bcol * gram * decay, 0.0)
            blocks.append(low[:128, :128])
            blocks.append(low[128:, 128:])
            lows.append(low[128:, :128])
            rhs.append(jnp.concatenate([key * (bcol * jnp.exp(ccol)), value * bcol], axis=1))

    def same(size):
        return (i128 // size) == (j128 // size)

    power = [jnp.where(same(8), -a, 0.0) for a in blocks]
    inv = [eye + a for a in power]
    for _ in range(2):
        power = [dot3(a, a) for a in power]
        inv = [b + dot3(b, a) for a, b in zip(power, inv)]
    for size in (8, 16, 32, 64):
        off = same(2 * size) & jnp.logical_not(same(size))
        mid = [dot3(jnp.where(off, a, 0.0), b) for a, b in zip(blocks, inv)]
        inv = [b - dot3(b, a) for a, b in zip(mid, inv)]

    first = [dot3(inv[2 * h], rhs[h][:128]) for h in range(4)]
    second = [rhs[h][128:] - dot3(lows[h], first[h]) for h in range(4)]
    second = [dot3(inv[2 * h + 1], second[h]) for h in range(4)]
    for h in range(4):
        wu = jnp.concatenate([first[h], second[h]], axis=0)
        wus[h] = wu
        last = crow[h : h + 1, TOK - 1 : TOK]
        k_dec = ks[h // 2] * jnp.exp(last - cols[:, h : h + 1])
        total = dot3(wu.T, k_dec)
        pair[k, h, 0:128, :] = (eye * (1.0 - jnp.exp(last)) + total[:128]).astype(BF16)
        pair[k, h, 128:256, :] = total[128:].astype(BF16)

    def l0_copy(h):
        return pltpu.make_async_remote_copy(
            src_ref=pair.at[k, h],
            dst_ref=pair.at[k, h],
            send_sem=l0_send.at[h],
            recv_sem=l0_recv.at[h],
            device_id=(c + 1 - 2 * k, y),
            device_id_type=MESH,
        )

    l0_copy(0).start()
    l0_copy(1).start()

    @pl.when(k == 0)
    def _():
        l0_copy(2).start()
        l0_copy(3).start()

    l0_copy(0).wait_recv()
    l0_copy(1).wait_recv()

    @pl.when(k == 1)
    def _():
        l0_copy(2).wait_recv()
        l0_copy(3).wait_recv()

    for j in range(2):
        h = 2 * k + j
        one, two = pair[0, h], pair[1, h]
        new = one.astype(F32) + two.astype(F32) - dot(one, two[:128])
        new = new.astype(BF16)
        comb[j, 0:64] = new[128:192]
        comb[j, 64:192] = new[0:128]
        comb[j, 192:256] = new[192:256]

    def p1_args(n):
        j, half = n // 2, n % 2
        return comb.at[j, pl.ds(64 * half, 192)], hbuf.at[z], 4 * k + n

    def p1_remote(n):
        src, dst, zz = p1_args(n)
        return pltpu.make_async_remote_copy(
            src_ref=src,
            dst_ref=dst,
            send_sem=p1_send.at[n],
            recv_sem=p1_recv.at[0],
            device_id=at(x, zz, k),
            device_id_type=MESH,
        )

    for n in range(4):

        @pl.when(z != 4 * k + n)
        def _():
            p1_remote(n).start()

        @pl.when(z == 4 * k + n)
        def _():
            src, dst, _ = p1_args(n)
            pltpu.make_async_copy(src, dst, p1_recv.at[0]).start()

    for g in range(2):
        qk = dot3(qs[g], ks[g], dot_nt)
        for r in range(2):
            h = 2 * g + r
            both_parts = dot3(qk * dec[h], wus[h])
            gs[h] = qs[g] * jnp.exp(cols[:, h : h + 1]) - both_parts[:, :128]
            os_[h] = both_parts[:, 128:]

    @pl.when(k == 1)
    def _():
        for h in range(4):
            moved = dot2(gs[h], pair[0, h], dot_nt)
            gs[h] = gs[h] - moved[:, :128]
            os_[h] = os_[h] + moved[:, 128:]

    def p2_copy(xx, sibling):
        if sibling:
            src = st.at[pl.ds(64, 64)]
            dst = xbuf.at[x, pl.ds(pl.multiple_of(128 * p, 64), 64)]
            target = at(xx, zs, k)
        else:
            rows = pl.ds(pl.multiple_of(64 * p, 64), 128)
            src, dst, target = st.at[rows], xbuf.at[x, rows], at(xx, z, k)
        return pltpu.make_async_remote_copy(
            src_ref=src,
            dst_ref=dst,
            send_sem=p2_send.at[2 * xx + sibling],
            recv_sem=p2_recv.at[x],
            device_id=target,
            device_id_type=MESH,
        )

    def p3_remote(i, kk):
        return pltpu.make_async_remote_copy(
            src_ref=obuf.at[i],
            dst_ref=sbuf.at[z // 2, pl.ds(pl.multiple_of(64 * p, 64), 64)],
            send_sem=p3_send.at[NC * i + kk],
            recv_sem=p3_recv.at[0],
            device_id=at(x, i, kk),
            device_id_type=MESH,
        )

    @pl.when(handler)
    def _():
        pltpu.make_async_copy(hbuf, hbuf, p1_recv.at[0]).wait()
        r_rows = pl.ds(pl.multiple_of(64 * (1 - p), 64), 128)
        s_rows = pl.ds(pl.multiple_of(128 * p, 64), 64)

        def leaf(i):
            return hbuf[i, r_rows], hbuf[i, s_rows]

        def leaf_stack(i):
            r, s = leaf(i)
            return jnp.concatenate([r, s], axis=0)

        def join(a, b):
            return a + b - dot3(a, b[:128])

        twos = []
        for i in range(0, 8, 2):
            a, b = leaf_stack(i), leaf_stack(i + 1)
            twos.append(a.astype(F32) + b.astype(F32) - dot(a, b[:128]))
        fours = [join(a, b) for a, b in zip(twos[::2], twos[1::2])]
        row = join(fours[0], fours[1])
        st[s_rows, :] = row[128:].astype(BF16)

        @pl.when(p == 0)
        def _():
            st[64:128, :] = row[0:64].astype(BF16)

        @pl.when(p == 1)
        def _():
            st[64:128, :] = row[64:128].astype(BF16)

        for xx in range(1, NX):

            @pl.when(x < xx)
            def _():
                p2_copy(xx, 0).start()
                p2_copy(xx, 1).start()

        def join_leaf(a, i):
            b = leaf_stack(i)
            return a + b.astype(F32) - dot2(a, b[:128])

        six = join(fours[0], twos[2])
        ahead = [
            leaf_stack(0).astype(F32),
            twos[0],
            join_leaf(twos[0], 2),
            fours[0],
            join_leaf(fours[0], 4),
            six,
            join_leaf(six, 6),
        ]
        for i in range(NZ - 1):
            ahead_n[i] = ahead[i][:128].astype(BF16)
            ahead_s[i] = ahead[i][128:]

        @pl.when(x == 0)
        def _():
            sin[...] = jnp.zeros((64, 128), F32)

        for o in range(NX - 1):

            @pl.when(x > o)
            def _():
                pltpu.make_async_copy(xbuf.at[o], xbuf.at[o], p2_recv.at[o]).wait()
                new = xbuf[o, s_rows].astype(F32)
                if o > 0:
                    now = sin[...]
                    new = now - dot2(now, xbuf[o, r_rows]) + new
                sin[...] = new

        s0 = sin[...]
        obuf[0] = s0.astype(BF16)
        for i in range(1, NZ):
            obuf[i] = (s0 - dot2(s0, ahead_n[i - 1]) + ahead_s[i - 1]).astype(BF16)
        for i in range(NZ):
            for kk in range(NC):
                me = (z == i) & (k == kk)

                @pl.when(jnp.logical_not(me))
                def _():
                    p3_remote(i, kk).start()

                @pl.when(me)
                def _():
                    pltpu.make_async_copy(
                        obuf.at[i],
                        sbuf.at[z // 2, pl.ds(pl.multiple_of(64 * p, 64), 64)],
                        p3_recv.at[0],
                    ).start()

    pltpu.make_async_copy(sbuf, sbuf, p3_recv.at[0]).wait()

    for h in range(4):
        g, r = h // 2, h % 2
        o = os_[h] + dot2(gs[h], sbuf[h], dot_nt)
        col = g * GROUP + 512 + r * 128
        gate = silu(pj[HALO : HALO + TOK, col : col + 128])
        mean = jnp.mean(o * o, axis=-1, keepdims=True)
        nrm[:, h * 128 : h * 128 + 128] = (
            o * lax.rsqrt(mean + EPS) * gain_ref[...] * gate
        ).astype(BF16)

    wo_copy.wait()

    def part(yy):
        rows = pl.ds(pl.multiple_of(64 * yy, 64), 64)
        return dot(nrm[rows, :], wo[...])

    def rs_copy(way, slot):
        n = 3 * way + slot
        return pltpu.make_async_remote_copy(
            src_ref=rst.at[n],
            dst_ref=rbuf.at[n],
            send_sem=rs_send.at[n],
            recv_sem=rs_recv.at[n],
            device_id=(c, up if way == 0 else down),
            device_id_type=MESH,
        )

    far = part(lax.rem(y + 2, ny)).astype(BF16)
    rst[0] = far[:32]
    rs_copy(0, 0).start()
    rst[3] = far[32:]
    rs_copy(1, 0).start()
    above = part(up)
    rst[1] = above[32:].astype(BF16)
    rs_copy(0, 1).start()
    beneath = part(down)
    rst[4] = beneath[:32].astype(BF16)
    rs_copy(1, 1).start()
    rs_copy(0, 0).wait_recv()
    rst[2] = (above[:32] + rbuf[0].astype(F32)).astype(BF16)
    rs_copy(0, 2).start()
    rs_copy(1, 0).wait_recv()
    rst[5] = (beneath[32:] + rbuf[3].astype(F32)).astype(BF16)
    rs_copy(1, 2).start()
    mine = part(y)
    rs_copy(0, 1).wait_recv()
    rs_copy(1, 1).wait_recv()
    top = mine[:32] + rbuf[4].astype(F32)
    low = mine[32:] + rbuf[1].astype(F32)
    rs_copy(0, 2).wait_recv()
    out_ref[:32] = (top + rbuf[2].astype(F32)).astype(BF16)
    rs_copy(1, 2).wait_recv()
    out_ref[32:] = (low + rbuf[5].astype(F32)).astype(BF16)

    for way in range(2):
        for half in range(2):
            ag_copy(way, half, 0).wait_send()
        ag_copy(way, way, 1).wait_send()
        for slot in range(3):
            rs_copy(way, slot).wait_send()

    @pl.when((y == ny - 1) & (c < nctx - 1))
    def _():
        for yy in range(ny):
            halo_copy(yy).wait_send()

    l0_copy(0).wait_send()
    l0_copy(1).wait_send()

    @pl.when(k == 0)
    def _():
        l0_copy(2).wait_send()
        l0_copy(3).wait_send()

    for n in range(4):

        @pl.when(z != 4 * k + n)
        def _():
            p1_remote(n).wait_send()

    @pl.when(handler)
    def _():
        for xx in range(1, NX):

            @pl.when(x < xx)
            def _():
                p2_copy(xx, 0).wait_send()
                p2_copy(xx, 1).wait_send()

        for i in range(NZ):
            for kk in range(NC):

                @pl.when(jnp.logical_not((z == i) & (k == kk)))
                def _():
                    p3_remote(i, kk).wait_send()


def local(ny, layer_in, in_proj, conv_weight, gate_logits, norm_gain, out_proj):
    rows, width = layer_in.shape
    vmem = pl.BlockSpec(memory_space=pltpu.VMEM)
    hbm = pl.BlockSpec(memory_space=pl.ANY)
    dma = pltpu.SemaphoreType.DMA
    return pl.pallas_call(
        functools.partial(kernel, ny),
        out_shape=jax.ShapeDtypeStruct((rows, width), BF16),
        in_specs=[hbm, hbm, vmem, vmem, vmem, hbm],
        out_specs=vmem,
        scratch_shapes=[
            pltpu.VMEM((HALO + TOK, width), BF16),
            pltpu.VMEM(in_proj.shape, BF16),
            pltpu.VMEM((width, 2 * GROUP), BF16),
            pltpu.VMEM((GROUP, 128), F32),
            pltpu.VMEM((HALO + TOK, 2 * GROUP), F32),
            pltpu.VMEM(out_proj.shape, BF16),
            pltpu.VMEM((2, TOK, 128), F32),
            pltpu.VMEM((2, TOK, 128), F32),
            pltpu.VMEM((4, TOK, TOK), F32),
            pltpu.VMEM((4, TOK, 256), F32),
            pltpu.VMEM((4, TOK, 128), F32),
            pltpu.VMEM((4, TOK, 128), F32),
            pltpu.VMEM((TOK, 512), BF16),
            pltpu.VMEM((2, 4, 256, 128), BF16),
            pltpu.VMEM((2, 256, 128), BF16),
            pltpu.VMEM((NZ, 192, 128), BF16),
            pltpu.VMEM((192, 128), BF16),
            pltpu.VMEM((NX, 192, 128), BF16),
            pltpu.VMEM((64, 128), F32),
            pltpu.VMEM((NZ, 64, 128), BF16),
            pltpu.VMEM((4, 128, 128), BF16),
            pltpu.VMEM((NZ - 1, 128, 128), BF16),
            pltpu.VMEM((NZ - 1, 64, 128), F32),
            pltpu.VMEM((6, 32, width), BF16),
            pltpu.VMEM((6, 32, width), BF16),
            pltpu.SemaphoreType.REGULAR((5,)),
            dma((4,)),
            dma((2,)),
            dma((6,)),
            dma((6,)),
            dma((4,)),
            dma((1,)),
            dma((4,)),
            dma((4,)),
            dma((4,)),
            dma((1,)),
            dma((2 * NX,)),
            dma((NX,)),
            dma((NZ * NC,)),
            dma((1,)),
            dma((6,)),
            dma((6,)),
        ],
        compiler_params=pltpu.CompilerParams(
            collective_id=0, has_side_effects=True, vmem_limit_bytes=56 << 20
        ),
    )(layer_in, in_proj, conv_weight, gate_logits, norm_gain.reshape(1, -1), out_proj)


def solution(mesh):
    in_specs = (
        P(("ctx", "head"), None),
        P(None, "head", None),
        P(None, "head", None),
        P(None, "head", "ctx"),
        P(),
        P("head", None),
    )
    out_specs = P(("ctx", "head"), None)
    return jax.shard_map(
        functools.partial(local, mesh.shape["head"]),
        mesh=mesh,
        in_specs=in_specs,
        out_specs=out_specs,
        check_vma=False,
    )
```

```python
import functools

import jax
import jax.numpy as jnp
from jax import lax
from jax.experimental import pallas as pl
from jax.experimental.pallas import tpu as pltpu
from jax.sharding import PartitionSpec as P

NX, NZ, NC = 4, 8, 2
DK = 128
GROUP = 768
TOK = 256
HALO = 16
EPS = 1e-06
MESH = pl.DeviceIdType.MESH
F32, BF16 = jnp.float32, jnp.bfloat16


def dot(a, b):
    return lax.dot_general(a, b, (((1,), (0,)), ((), ())), preferred_element_type=F32)


def dot_nt(a, b):
    return lax.dot_general(a, b, (((1,), (1,)), ((), ())), preferred_element_type=F32)


def split(a):
    hi = a.astype(BF16)
    return hi, (a - hi.astype(F32)).astype(BF16)


def dot3(a, b, op=dot):
    ah, al = split(a)
    bh, bl = split(b)
    return op(ah, bh) + (op(al, bh) + op(ah, bl))


def dot2(a, b, op=dot):
    ah, al = split(a)
    return op(ah, b) + op(al, b)


def iota(shape, dim):
    return lax.broadcasted_iota(jnp.int32, shape, dim)


def silu(a):
    return a * jax.nn.sigmoid(a)


def log1p(u):
    series = u * (1.0 - u * (0.5 - u * (1.0 / 3.0 - u * 0.25)))
    return jnp.where(u < 1.0 / 64.0, series, jnp.log(1.0 + u))


def kernel(
    ny,
    x_ref,
    w_ref,
    cw_ref,
    gate_ref,
    gain_ref,
    wo_ref,
    out_ref,
    xg,
    w3,
    w2,
    tmp,
    pj,
    wo,
    qs,
    ks,
    dec,
    wus,
    gs,
    os_,
    nrm,
    pair,
    comb,
    hbuf,
    st,
    xbuf,
    sin,
    obuf,
    sbuf,
    ahead_n,
    ahead_s,
    rst,
    rbuf,
    round_sem,
    w_sem,
    loc_sem,
    ag_send,
    ag_recv,
    halo_send,
    halo_recv,
    l0_send,
    l0_recv,
    p1_send,
    p1_recv,
    p2_send,
    p2_recv,
    p3_send,
    p3_recv,
    rs_send,
    rs_recv,
):
    c = lax.axis_index("ctx")
    y = lax.axis_index("head")
    nctx = NX * NZ * NC
    k = lax.rem(c, NC)
    z = lax.rem(c // NC, NZ)
    x = c // (NC * NZ)
    handler = (k == z // (NZ // NC)) & (lax.rem(z, 2) == 0)

    def at(xx, zz, kk):
        return ((xx * NZ + zz) * NC + kk, y)

    xg[0:HALO, :] = jnp.zeros((HALO, xg.shape[1]), BF16)

    rows_w = w3.shape[0] // 4
    w_copies = []
    for i in range(4):
        part = pl.ds(i * rows_w, rows_w)
        w_copies.append(pltpu.make_async_copy(w_ref.at[part], w3.at[part], w_sem.at[i]))
        w_copies[-1].start()
    own_rows = pl.ds(pl.multiple_of(HALO + 64 * y, 16), 64)
    own_x = pltpu.make_async_copy(x_ref, xg.at[own_rows], loc_sem.at[0])
    own_x.start()

    barrier = pltpu.get_barrier_semaphore()

    def hello(target):
        pl.semaphore_signal(barrier, inc=1, device_id=target, device_id_type=MESH)

    up, down = lax.rem(y + 1, ny), lax.rem(y + ny - 1, ny)
    hello((c, up))
    hello((c, down))
    hello((lax.rem(c + 1, nctx), y))
    hello((lax.rem(c + nctx - 1, nctx), y))

    @pl.when(c > 0)
    def _():
        hello((c - 1, ny - 1))

    halo_out = jnp.where((y == ny - 1) & (c < nctx - 1), ny, 0)
    pl.semaphore_wait(barrier, 4 + halo_out)

    def tell(n):
        for step in (2**n, nctx - 2**n):
            pl.semaphore_signal(
                round_sem.at[n],
                inc=1,
                device_id=(lax.rem(c + step, nctx), y),
                device_id_type=MESH,
            )

    def wider(n):
        pl.semaphore_wait(round_sem.at[n], 2)
        if n < 4:
            tell(n + 1)

    def block_rows(yy, half):
        return pl.ds(pl.multiple_of(HALO + 64 * yy + 32 * half, 16), 32)

    def ag_copy(way, half, hop):
        owner = y if hop == 0 else (down if way == 0 else up)
        src = x_ref.at[pl.ds(32 * half, 32)] if hop == 0 else xg.at[block_rows(owner, half)]
        n = 3 * way + (2 if hop else (half if way == 0 else 1 - half))
        return pltpu.make_async_remote_copy(
            src_ref=src,
            dst_ref=xg.at[block_rows(owner, half)],
            send_sem=ag_send.at[n],
            recv_sem=ag_recv.at[n],
            device_id=(c, up if way == 0 else down),
            device_id_type=MESH,
        )

    def halo_copy(yy):
        return pltpu.make_async_remote_copy(
            src_ref=x_ref.at[pl.ds(64 - 8, 8)],
            dst_ref=xg.at[pl.ds(HALO - 8, 8)],
            send_sem=halo_send.at[yy],
            recv_sem=halo_recv.at[0],
            device_id=(c + 1, yy),
            device_id_type=MESH,
        )

    ag_copy(0, 0, 0).start()
    ag_copy(1, 1, 0).start()
    ag_copy(0, 1, 0).start()
    ag_copy(1, 0, 0).start()

    @pl.when((y == ny - 1) & (c < nctx - 1))
    def _():
        for yy in range(ny):
            halo_copy(yy).start()

    tell(0)
    wo_copy = pltpu.make_async_copy(wo_ref, wo, loc_sem.at[1])
    wo_copy.start()

    w2d = w3.reshape(2 * w3.shape[0], GROUP)
    for i in range(4):
        w_copies[i].wait()

        @pl.loop(i * rows_w // 64, (i + 1) * rows_w // 64)
        def _(s):
            r = pl.ds(pl.multiple_of(s * 64, 64), 64)
            r2 = pl.ds(pl.multiple_of(s * 128, 128), 128)
            for b in range(0, GROUP, 128):
                tmp[b : b + 128, :] = w2d[r2, b : b + 128].astype(F32)
            for g in range(2):
                for b in range(0, GROUP, 128):
                    piece = tmp[pl.ds(b + g, 64, stride=2), :]
                    w2[r, g * GROUP + b : g * GROUP + b + 128] = piece.astype(BF16)

        if i == 3:
            wider(0)
        if i == 1:
            ag_copy(0, 0, 0).wait_recv()
            ag_copy(0, 0, 1).start()
            ag_copy(1, 1, 0).wait_recv()
            ag_copy(1, 1, 1).start()


    alog = gate_ref[0]
    log_decay = -(jnp.maximum(alog, 0.0) + log1p(jnp.exp(-jnp.abs(alog))))
    beta_row = jax.nn.sigmoid(gate_ref[1])
    both = jnp.concatenate([log_decay, beta_row], axis=0)
    upper = (iota((TOK, TOK), 0) <= iota((TOK, TOK), 1)).astype(F32)
    crow = jnp.dot(both, upper, precision=lax.Precision.HIGHEST, preferred_element_type=F32)
    cols = jnp.concatenate([crow[:4], beta_row], axis=0).T

    def project(start, count):
        rows = pl.ds(start if count == HALO else pl.multiple_of(HALO + 64 * start, 16), count)
        for b in range(0, 2 * GROUP, 512):
            pj[rows, b : b + 512] = dot(xg[rows, :], w2[:, b : b + 512]).astype(BF16).astype(F32)

    own_x.wait()
    project(y, 64)

    @pl.when(c > 0)
    def _():
        halo_copy(0).wait_recv()

    project(0, HALO)
    ag_copy(0, 1, 0).wait_recv()
    project(down, 64)
    ag_copy(1, 0, 0).wait_recv()
    project(up, 64)
    ag_copy(0, 0, 1).wait_recv()
    ag_copy(1, 1, 1).wait_recv()
    project(lax.rem(y + 2, ny), 64)

    wider(1)

    def conv(g, b):
        col = g * GROUP + b * 128
        total = None
        for i in range(4):
            w = cw_ref[i, pl.ds(g, 1), b * 128 : b * 128 + 128]
            term = pj[HALO - 3 + i : HALO - 3 + i + TOK, col : col + 128] * w
            total = term if total is None else total + term
        return silu(total)

    def unit(u):
        return u * lax.rsqrt(jnp.sum(u * u, axis=-1, keepdims=True) + EPS)

    below = iota((TOK, TOK), 0) > iota((TOK, TOK), 1)
    on_or_below = iota((TOK, TOK), 0) >= iota((TOK, TOK), 1)
    i128, j128 = iota((128, 128), 0), iota((128, 128), 1)
    eye = (i128 == j128).astype(F32)

    blocks, lows, rhs = [], [], []
    for g in range(2):
        qs[g] = unit(conv(g, 0)) * (DK**-0.5)
        key = unit(conv(g, 1))
        ks[g] = key
        gram = dot3(key, key, dot_nt)
        for r in range(2):
            h = 2 * g + r
            value = conv(g, 2 + r)
            ccol, bcol = cols[:, h : h + 1], cols[:, 4 + h : 5 + h]
            gap = ccol - crow[h : h + 1, :]
            decay = jnp.where(on_or_below, jnp.exp(jnp.where(on_or_below, gap, 0.0)), 0.0)
            dec[h] = decay
            low = jnp.where(below, bcol * gram * decay, 0.0)
            blocks.append(low[:128, :128])
            blocks.append(low[128:, 128:])
            lows.append(low[128:, :128])
            rhs.append(jnp.concatenate([key * (bcol * jnp.exp(ccol)), value * bcol], axis=1))

    wider(2)

    def same(size):
        return (i128 // size) == (j128 // size)

    power = [jnp.where(same(8), -a, 0.0) for a in blocks]
    inv = [eye + a for a in power]
    for _ in range(2):
        power = [dot3(a, a) for a in power]
        inv = [b + dot3(b, a) for a, b in zip(power, inv)]
    for size in (8, 16, 32, 64):
        off = same(2 * size) & jnp.logical_not(same(size))
        mid = [dot3(jnp.where(off, a, 0.0), b) for a, b in zip(blocks, inv)]
        inv = [b - dot3(b, a) for a, b in zip(mid, inv)]

    first = [dot3(inv[2 * h], rhs[h][:128]) for h in range(4)]
    second = [rhs[h][128:] - dot3(lows[h], first[h]) for h in range(4)]
    second = [dot3(inv[2 * h + 1], second[h]) for h in range(4)]
    for h in range(4):
        wu = jnp.concatenate([first[h], second[h]], axis=0)
        wus[h] = wu
        last = crow[h : h + 1, TOK - 1 : TOK]
        k_dec = ks[h // 2] * jnp.exp(last - cols[:, h : h + 1])
        total = dot3(wu.T, k_dec)
        pair[k, h, 0:128, :] = (eye * (1.0 - jnp.exp(last)) + total[:128]).astype(BF16)
        pair[k, h, 128:256, :] = total[128:].astype(BF16)

    wider(3)

    def l0_copy(h):
        return pltpu.make_async_remote_copy(
            src_ref=pair.at[k, h],
            dst_ref=pair.at[k, h],
            send_sem=l0_send.at[h],
            recv_sem=l0_recv.at[h],
            device_id=(c + 1 - 2 * k, y),
            device_id_type=MESH,
        )

    l0_copy(0).start()
    l0_copy(1).start()

    @pl.when(k == 0)
    def _():
        l0_copy(2).start()
        l0_copy(3).start()

    l0_copy(0).wait_recv()
    l0_copy(1).wait_recv()

    @pl.when(k == 1)
    def _():
        l0_copy(2).wait_recv()
        l0_copy(3).wait_recv()

    for j in range(2):
        h = 2 * k + j
        one, two = pair[0, h], pair[1, h]
        new = one.astype(F32) + two.astype(F32) - dot(one, two[:128])
        comb[j] = new.astype(BF16)

    def p1_remote(j):
        return pltpu.make_async_remote_copy(
            src_ref=comb.at[j],
            dst_ref=hbuf.at[z],
            send_sem=p1_send.at[j],
            recv_sem=p1_recv.at[0],
            device_id=at(x, 4 * k + 2 * j, k),
            device_id_type=MESH,
        )

    for j in range(2):

        @pl.when(z != 4 * k + 2 * j)
        def _():
            p1_remote(j).start()

        @pl.when(z == 4 * k + 2 * j)
        def _():
            pltpu.make_async_copy(comb.at[j], hbuf.at[z], p1_recv.at[0]).start()

    for g in range(2):
        qk = dot3(qs[g], ks[g], dot_nt)
        for r in range(2):
            h = 2 * g + r
            both_parts = dot3(qk * dec[h], wus[h])
            gs[h] = qs[g] * jnp.exp(cols[:, h : h + 1]) - both_parts[:, :128]
            os_[h] = both_parts[:, 128:]

    @pl.when(k == 1)
    def _():
        for h in range(4):
            moved = dot2(gs[h], pair[0, h], dot_nt)
            gs[h] = gs[h] - moved[:, :128]
            os_[h] = os_[h] + moved[:, 128:]

    wider(4)

    def p2_copy(xx):
        return pltpu.make_async_remote_copy(
            src_ref=st,
            dst_ref=xbuf.at[x],
            send_sem=p2_send.at[xx],
            recv_sem=p2_recv.at[x],
            device_id=at(xx, z, k),
            device_id_type=MESH,
        )

    def p3_remote(i, kk):
        return pltpu.make_async_remote_copy(
            src_ref=obuf.at[i],
            dst_ref=sbuf.at[z // 2],
            send_sem=p3_send.at[NC * i + kk],
            recv_sem=p3_recv.at[0],
            device_id=at(x, i, kk),
            device_id_type=MESH,
        )

    @pl.when(handler)
    def _():
        pltpu.make_async_copy(hbuf, hbuf, p1_recv.at[0]).wait()
        def join(a, b):
            return a + b - dot2(a, b[:128].astype(BF16))

        twos = []
        for i in range(0, 8, 2):
            a, b = hbuf[i], hbuf[i + 1]
            twos.append(a.astype(F32) + b.astype(F32) - dot(a, b[:128]))
        fours = [join(a, b) for a, b in zip(twos[::2], twos[1::2])]
        row = join(fours[0], fours[1])
        st[...] = row.astype(BF16)
        for xx in range(1, NX):

            @pl.when(x < xx)
            def _():
                p2_copy(xx).start()

        def join_leaf(a, i):
            b = hbuf[i]
            return a + b.astype(F32) - dot2(a, b[:128])

        six = join(fours[0], twos[2])
        ahead = [
            hbuf[0].astype(F32),
            twos[0],
            join_leaf(twos[0], 2),
            fours[0],
            join_leaf(fours[0], 4),
            six,
            join_leaf(six, 6),
        ]
        for i in range(NZ - 1):
            ahead_n[i] = ahead[i][:128].astype(BF16)
            ahead_s[i] = ahead[i][128:]

        @pl.when(x == 0)
        def _():
            sin[...] = jnp.zeros((128, 128), F32)

        for o in range(NX - 1):

            @pl.when(x > o)
            def _():
                pltpu.make_async_copy(xbuf.at[o], xbuf.at[o], p2_recv.at[o]).wait()
                new = xbuf[o, 128:].astype(F32)
                if o > 0:
                    now = sin[...]
                    new = now - dot2(now, xbuf[o, :128]) + new
                sin[...] = new

        s0 = sin[...]
        obuf[0] = s0.astype(BF16)
        for i in range(1, NZ):
            obuf[i] = (s0 - dot2(s0, ahead_n[i - 1]) + ahead_s[i - 1]).astype(BF16)
        for i in range(NZ):
            for kk in range(NC):
                me = (z == i) & (k == kk)

                @pl.when(jnp.logical_not(me))
                def _():
                    p3_remote(i, kk).start()

                @pl.when(me)
                def _():
                    pltpu.make_async_copy(obuf.at[i], sbuf.at[z // 2], p3_recv.at[0]).start()

    pltpu.make_async_copy(sbuf, sbuf, p3_recv.at[0]).wait()

    for h in range(4):
        g, r = h // 2, h % 2
        o = os_[h] + dot2(gs[h], sbuf[h], dot_nt)
        col = g * GROUP + 512 + r * 128
        gate = silu(pj[HALO : HALO + TOK, col : col + 128])
        mean = jnp.mean(o * o, axis=-1, keepdims=True)
        nrm[:, h * 128 : h * 128 + 128] = (
            o * lax.rsqrt(mean + EPS) * gain_ref[...] * gate
        ).astype(BF16)

    wo_copy.wait()

    def part(yy):
        rows = pl.ds(pl.multiple_of(64 * yy, 64), 64)
        return dot(nrm[rows, :], wo[...])

    def rs_copy(way, slot):
        n = 3 * way + slot
        return pltpu.make_async_remote_copy(
            src_ref=rst.at[n],
            dst_ref=rbuf.at[n],
            send_sem=rs_send.at[n],
            recv_sem=rs_recv.at[n],
            device_id=(c, up if way == 0 else down),
            device_id_type=MESH,
        )

    far = part(lax.rem(y + 2, ny)).astype(BF16)
    rst[0] = far[:32]
    rs_copy(0, 0).start()
    rst[3] = far[32:]
    rs_copy(1, 0).start()
    above = part(up)
    rst[1] = above[32:].astype(BF16)
    rs_copy(0, 1).start()
    beneath = part(down)
    rst[4] = beneath[:32].astype(BF16)
    rs_copy(1, 1).start()
    rs_copy(0, 0).wait_recv()
    rst[2] = (above[:32] + rbuf[0].astype(F32)).astype(BF16)
    rs_copy(0, 2).start()
    rs_copy(1, 0).wait_recv()
    rst[5] = (beneath[32:] + rbuf[3].astype(F32)).astype(BF16)
    rs_copy(1, 2).start()
    mine = part(y)
    rs_copy(0, 1).wait_recv()
    rs_copy(1, 1).wait_recv()
    top = mine[:32] + rbuf[4].astype(F32)
    low = mine[32:] + rbuf[1].astype(F32)
    rs_copy(0, 2).wait_recv()
    out_ref[:32] = (top + rbuf[2].astype(F32)).astype(BF16)
    rs_copy(1, 2).wait_recv()
    out_ref[32:] = (low + rbuf[5].astype(F32)).astype(BF16)

    for way in range(2):
        for half in range(2):
            ag_copy(way, half, 0).wait_send()
        ag_copy(way, way, 1).wait_send()
        for slot in range(3):
            rs_copy(way, slot).wait_send()

    @pl.when((y == ny - 1) & (c < nctx - 1))
    def _():
        for yy in range(ny):
            halo_copy(yy).wait_send()

    l0_copy(0).wait_send()
    l0_copy(1).wait_send()

    @pl.when(k == 0)
    def _():
        l0_copy(2).wait_send()
        l0_copy(3).wait_send()

    for j in range(2):

        @pl.when(z != 4 * k + 2 * j)
        def _():
            p1_remote(j).wait_send()

    @pl.when(handler)
    def _():
        for xx in range(1, NX):

            @pl.when(x < xx)
            def _():
                p2_copy(xx).wait_send()

        for i in range(NZ):
            for kk in range(NC):

                @pl.when(jnp.logical_not((z == i) & (k == kk)))
                def _():
                    p3_remote(i, kk).wait_send()


def local(ny, layer_in, in_proj, conv_weight, gate_logits, norm_gain, out_proj):
    rows, width = layer_in.shape
    vmem = pl.BlockSpec(memory_space=pltpu.VMEM)
    hbm = pl.BlockSpec(memory_space=pl.ANY)
    dma = pltpu.SemaphoreType.DMA
    return pl.pallas_call(
        functools.partial(kernel, ny),
        out_shape=jax.ShapeDtypeStruct((rows, width), BF16),
        in_specs=[hbm, hbm, vmem, vmem, vmem, hbm],
        out_specs=vmem,
        scratch_shapes=[
            pltpu.VMEM((HALO + TOK, width), BF16),
            pltpu.VMEM(in_proj.shape, BF16),
            pltpu.VMEM((width, 2 * GROUP), BF16),
            pltpu.VMEM((GROUP, 128), F32),
            pltpu.VMEM((HALO + TOK, 2 * GROUP), F32),
            pltpu.VMEM(out_proj.shape, BF16),
            pltpu.VMEM((2, TOK, 128), F32),
            pltpu.VMEM((2, TOK, 128), F32),
            pltpu.VMEM((4, TOK, TOK), F32),
            pltpu.VMEM((4, TOK, 256), F32),
            pltpu.VMEM((4, TOK, 128), F32),
            pltpu.VMEM((4, TOK, 128), F32),
            pltpu.VMEM((TOK, 512), BF16),
            pltpu.VMEM((2, 4, 256, 128), BF16),
            pltpu.VMEM((2, 256, 128), BF16),
            pltpu.VMEM((NZ, 256, 128), BF16),
            pltpu.VMEM((256, 128), BF16),
            pltpu.VMEM((NX, 256, 128), BF16),
            pltpu.VMEM((128, 128), F32),
            pltpu.VMEM((NZ, 128, 128), BF16),
            pltpu.VMEM((4, 128, 128), BF16),
            pltpu.VMEM((NZ - 1, 128, 128), BF16),
            pltpu.VMEM((NZ - 1, 128, 128), F32),
            pltpu.VMEM((6, 32, width), BF16),
            pltpu.VMEM((6, 32, width), BF16),
            pltpu.SemaphoreType.REGULAR((5,)),
            dma((4,)),
            dma((2,)),
            dma((6,)),
            dma((6,)),
            dma((4,)),
            dma((1,)),
            dma((4,)),
            dma((4,)),
            dma((4,)),
            dma((1,)),
            dma((2 * NX,)),
            dma((NX,)),
            dma((NZ * NC,)),
            dma((1,)),
            dma((6,)),
            dma((6,)),
        ],
        compiler_params=pltpu.CompilerParams(
            collective_id=0, has_side_effects=True, vmem_limit_bytes=56 << 20
        ),
    )(layer_in, in_proj, conv_weight, gate_logits, norm_gain.reshape(1, -1), out_proj)


def solution(mesh):
    in_specs = (
        P(("ctx", "head"), None),
        P(None, "head", None),
        P(None, "head", None),
        P(None, "head", "ctx"),
        P(),
        P("head", None),
    )
    out_specs = P(("ctx", "head"), None)
    return jax.shard_map(
        functools.partial(local, mesh.shape["head"]),
        mesh=mesh,
        in_specs=in_specs,
        out_specs=out_specs,
        check_vma=False,
    )
```

```python
import functools

import jax
import jax.numpy as jnp
from jax import lax
from jax.experimental import pallas as pl
from jax.experimental.pallas import tpu as pltpu
from jax.sharding import PartitionSpec as P

NX, NZ, NC = 4, 8, 2
DK = 128
GROUP = 768
TOK = 256
HALO = 16
EPS = 1e-06
MESH = pl.DeviceIdType.MESH
F32, BF16 = jnp.float32, jnp.bfloat16


def dot(a, b):
    return lax.dot_general(a, b, (((1,), (0,)), ((), ())), preferred_element_type=F32)


def dot_nt(a, b):
    return lax.dot_general(a, b, (((1,), (1,)), ((), ())), preferred_element_type=F32)


def split(a):
    hi = a.astype(BF16)
    return hi, (a - hi.astype(F32)).astype(BF16)


def dot3(a, b):
    ah, al = split(a)
    bh, bl = split(b)
    if a.shape[1] != 128:
        return dot(ah, bh) + (dot(al, bh) + dot(ah, bl))
    left = jnp.concatenate([ah, al], axis=1)
    if b.shape[1] != 128:
        return dot(left, jnp.concatenate([bh, bh], axis=0)) + dot(ah, bl)
    upper = jnp.concatenate([bh, bl], axis=1)
    lower = jnp.concatenate([bh, jnp.zeros_like(bh)], axis=1)
    wide = dot(left, jnp.concatenate([upper, lower], axis=0))
    return wide[:, :128] + wide[:, 128:]


def dot3_nt(a, b):
    ah, al = split(a)
    bh, bl = split(b)
    left, right = jnp.concatenate([ah, al], axis=1), jnp.concatenate([bh, bh], axis=1)
    return dot_nt(left, right) + dot_nt(ah, bl)


def dot2(a, b):
    ah, al = split(a)
    return dot(jnp.concatenate([ah, al], axis=1), jnp.concatenate([b, b], axis=0))


def dot2_nt(a, b):
    ah, al = split(a)
    return dot_nt(jnp.concatenate([ah, al], axis=1), jnp.concatenate([b, b], axis=1))


def iota(shape, dim):
    return lax.broadcasted_iota(jnp.int32, shape, dim)


def silu(a):
    return a * jax.nn.sigmoid(a)


def log1p(u):
    series = u * (1.0 - u * (0.5 - u * (1.0 / 3.0 - u * 0.25)))
    return jnp.where(u < 1.0 / 64.0, series, jnp.log(1.0 + u))


def kernel(
    ny,
    x_ref,
    w_ref,
    cw_ref,
    gate_ref,
    gain_ref,
    wo_ref,
    out_ref,
    xg,
    w3,
    w2,
    tmp,
    pj,
    wo,
    qs,
    ks,
    dec,
    wus,
    gs,
    os_,
    gz,
    pair,
    comb,
    hbuf,
    st,
    xbuf,
    sin,
    obuf,
    sbuf,
    ahead_n,
    ahead_s,
    rst,
    rbuf,
    round_sem,
    w_sem,
    loc_sem,
    ag_send,
    ag_recv,
    halo_send,
    halo_recv,
    l0_send,
    l0_recv,
    p1_send,
    p1_recv,
    p2_send,
    p2_recv,
    p3_send,
    p3_recv,
    rs_send,
    rs_recv,
):
    c = lax.axis_index("ctx")
    y = lax.axis_index("head")
    nctx = NX * NZ * NC
    k = lax.rem(c, NC)
    z = lax.rem(c // NC, NZ)
    x = c // (NC * NZ)
    handler = (k == z // (NZ // NC)) & (lax.rem(z, 2) == 0)

    def at(xx, zz, kk):
        return ((xx * NZ + zz) * NC + kk, y)

    xg[0:HALO, :] = jnp.zeros((HALO, xg.shape[1]), BF16)

    rows_w = w3.shape[0] // 4
    w_copies = []
    for i in range(4):
        part = pl.ds(i * rows_w, rows_w)
        w_copies.append(pltpu.make_async_copy(w_ref.at[part], w3.at[part], w_sem.at[i]))
        w_copies[-1].start()
    own_rows = pl.ds(pl.multiple_of(HALO + 64 * y, 16), 64)
    own_x = pltpu.make_async_copy(x_ref, xg.at[own_rows], loc_sem.at[0])
    own_x.start()

    barrier = pltpu.get_barrier_semaphore()

    def hello(target):
        pl.semaphore_signal(barrier, inc=1, device_id=target, device_id_type=MESH)

    up, down = lax.rem(y + 1, ny), lax.rem(y + ny - 1, ny)
    hello((c, up))
    hello((c, down))
    hello((lax.rem(c + 1, nctx), y))
    hello((lax.rem(c + nctx - 1, nctx), y))

    @pl.when(c > 0)
    def _():
        hello((c - 1, ny - 1))

    halo_out = jnp.where((y == ny - 1) & (c < nctx - 1), ny, 0)
    pl.semaphore_wait(barrier, 4 + halo_out)

    def tell(n):
        for step in (2**n, nctx - 2**n):
            pl.semaphore_signal(
                round_sem.at[n],
                inc=1,
                device_id=(lax.rem(c + step, nctx), y),
                device_id_type=MESH,
            )

    def wider(n):
        pl.semaphore_wait(round_sem.at[n], 2)
        if n < 4:
            tell(n + 1)

    def block_rows(yy, half):
        return pl.ds(pl.multiple_of(HALO + 64 * yy + 32 * half, 16), 32)

    def ag_copy(way, half, hop):
        owner = y if hop == 0 else (down if way == 0 else up)
        src = x_ref.at[pl.ds(32 * half, 32)] if hop == 0 else xg.at[block_rows(owner, half)]
        n = 3 * way + (2 if hop else (half if way == 0 else 1 - half))
        return pltpu.make_async_remote_copy(
            src_ref=src,
            dst_ref=xg.at[block_rows(owner, half)],
            send_sem=ag_send.at[n],
            recv_sem=ag_recv.at[n],
            device_id=(c, up if way == 0 else down),
            device_id_type=MESH,
        )

    def halo_copy(yy):
        return pltpu.make_async_remote_copy(
            src_ref=x_ref.at[pl.ds(64 - 8, 8)],
            dst_ref=xg.at[pl.ds(HALO - 8, 8)],
            send_sem=halo_send.at[yy],
            recv_sem=halo_recv.at[0],
            device_id=(c + 1, yy),
            device_id_type=MESH,
        )

    ag_copy(0, 0, 0).start()
    ag_copy(1, 1, 0).start()
    ag_copy(0, 1, 0).start()
    ag_copy(1, 0, 0).start()

    @pl.when((y == ny - 1) & (c < nctx - 1))
    def _():
        for yy in range(ny):
            halo_copy(yy).start()

    tell(0)
    wo_copy = pltpu.make_async_copy(wo_ref, wo, loc_sem.at[1])
    wo_copy.start()

    w2d = w3.reshape(2 * w3.shape[0], GROUP)
    for i in range(4):
        w_copies[i].wait()

        @pl.loop(i * rows_w // 64, (i + 1) * rows_w // 64)
        def _(s):
            r = pl.ds(pl.multiple_of(s * 64, 64), 64)
            r2 = pl.ds(pl.multiple_of(s * 128, 128), 128)
            for b in range(0, GROUP, 128):
                tmp[b : b + 128, :] = w2d[r2, b : b + 128].astype(F32)
            for g in range(2):
                for b in range(0, GROUP, 128):
                    piece = tmp[pl.ds(b + g, 64, stride=2), :]
                    w2[r, g * GROUP + b : g * GROUP + b + 128] = piece.astype(BF16)

        if i == 3:
            wider(0)
        if i == 1:
            ag_copy(0, 0, 0).wait_recv()
            ag_copy(0, 0, 1).start()
            ag_copy(1, 1, 0).wait_recv()
            ag_copy(1, 1, 1).start()


    alog = gate_ref[0]
    log_decay = -(jnp.maximum(alog, 0.0) + log1p(jnp.exp(-jnp.abs(alog))))
    beta_row = jax.nn.sigmoid(gate_ref[1])
    both = jnp.concatenate([log_decay, beta_row], axis=0)
    upper = (iota((TOK, TOK), 0) <= iota((TOK, TOK), 1)).astype(F32)
    crow = jnp.dot(both, upper, precision=lax.Precision.HIGHEST, preferred_element_type=F32)
    cols = jnp.concatenate([crow[:4], beta_row], axis=0).T

    own_x.wait()
    ag_copy(0, 1, 0).wait_recv()
    ag_copy(1, 0, 0).wait_recv()

    @pl.when(c > 0)
    def _():
        halo_copy(0).wait_recv()

    ag_copy(0, 0, 1).wait_recv()
    ag_copy(1, 1, 1).wait_recv()
    for b in range(0, 2 * GROUP, 512):
        pj[:, b : b + 512] = dot(xg[...], w2[:, b : b + 512]).astype(BF16).astype(F32)

    wider(1)

    def conv(g, b):
        col = g * GROUP + b * 128
        total = None
        for i in range(4):
            w = cw_ref[i, pl.ds(g, 1), b * 128 : b * 128 + 128]
            term = pj[HALO - 3 + i : HALO - 3 + i + TOK, col : col + 128] * w
            total = term if total is None else total + term
        return silu(total)

    def unit(u):
        return u * lax.rsqrt(jnp.sum(u * u, axis=-1, keepdims=True) + EPS)

    below = iota((TOK, TOK), 0) > iota((TOK, TOK), 1)
    on_or_below = iota((TOK, TOK), 0) >= iota((TOK, TOK), 1)
    i128, j128 = iota((128, 128), 0), iota((128, 128), 1)
    eye = (i128 == j128).astype(F32)

    blocks, lows, rhs = [], [], []
    for g in range(2):
        qs[g] = unit(conv(g, 0)) * (DK**-0.5)
        key = unit(conv(g, 1))
        ks[g] = key
        gram = dot3_nt(key, key)
        for r in range(2):
            h = 2 * g + r
            value = conv(g, 2 + r)
            ccol, bcol = cols[:, h : h + 1], cols[:, 4 + h : 5 + h]
            gap = ccol - crow[h : h + 1, :]
            decay = jnp.where(on_or_below, jnp.exp(jnp.where(on_or_below, gap, 0.0)), 0.0)
            dec[h] = decay
            low = jnp.where(below, bcol * gram * decay, 0.0)
            blocks.append(low[:128, :128])
            blocks.append(low[128:, 128:])
            lows.append(low[128:, :128])
            rhs.append(jnp.concatenate([key * (bcol * jnp.exp(ccol)), value * bcol], axis=1))

    wider(2)

    def same(size):
        return (i128 // size) == (j128 // size)

    power = [jnp.where(same(8), -a, 0.0) for a in blocks]
    inv = [eye + a for a in power]
    for _ in range(2):
        power = [dot3(a, a) for a in power]
        inv = [b + dot3(b, a) for a, b in zip(power, inv)]
    for size in (8, 16, 32, 64):
        off = same(2 * size) & jnp.logical_not(same(size))
        mid = [dot3(jnp.where(off, a, 0.0), b) for a, b in zip(blocks, inv)]
        inv = [b - dot3(b, a) for a, b in zip(mid, inv)]

    first = [dot3(inv[2 * h], rhs[h][:128]) for h in range(4)]
    second = [rhs[h][128:] - dot3(lows[h], first[h]) for h in range(4)]
    second = [dot3(inv[2 * h + 1], second[h]) for h in range(4)]
    for h in range(4):
        wu = jnp.concatenate([first[h], second[h]], axis=0)
        wus[h] = wu
        last = crow[h : h + 1, TOK - 1 : TOK]
        k_dec = ks[h // 2] * jnp.exp(last - cols[:, h : h + 1])
        total = dot3(wu.T, k_dec)
        pair[k, h, 0:128, :] = (eye * (1.0 - jnp.exp(last)) + total[:128]).astype(BF16)
        pair[k, h, 128:256, :] = total[128:].astype(BF16)

    wider(3)

    def l0_copy(h):
        return pltpu.make_async_remote_copy(
            src_ref=pair.at[k, h],
            dst_ref=pair.at[k, h],
            send_sem=l0_send.at[h],
            recv_sem=l0_recv.at[h],
            device_id=(c + 1 - 2 * k, y),
            device_id_type=MESH,
        )

    l0_copy(0).start()
    l0_copy(1).start()

    @pl.when(k == 0)
    def _():
        l0_copy(2).start()
        l0_copy(3).start()

    l0_copy(0).wait_recv()
    l0_copy(1).wait_recv()

    @pl.when(k == 1)
    def _():
        l0_copy(2).wait_recv()
        l0_copy(3).wait_recv()

    for j in range(2):
        h = 2 * k + j
        one, two = pair[0, h], pair[1, h]
        new = one.astype(F32) + two.astype(F32) - dot(one, two[:128])
        comb[j] = new.astype(BF16)

    def p1_remote(j):
        return pltpu.make_async_remote_copy(
            src_ref=comb.at[j],
            dst_ref=hbuf.at[z],
            send_sem=p1_send.at[j],
            recv_sem=p1_recv.at[0],
            device_id=at(x, 4 * k + 2 * j, k),
            device_id_type=MESH,
        )

    for j in range(2):

        @pl.when(z != 4 * k + 2 * j)
        def _():
            p1_remote(j).start()

        @pl.when(z == 4 * k + 2 * j)
        def _():
            pltpu.make_async_copy(comb.at[j], hbuf.at[z], p1_recv.at[0]).start()

    for g in range(2):
        qk = dot3_nt(qs[g], ks[g])
        for r in range(2):
            h = 2 * g + r
            both_parts = dot3(qk * dec[h], wus[h])
            gs[h] = qs[g] * jnp.exp(cols[:, h : h + 1]) - both_parts[:, :128]
            os_[h] = both_parts[:, 128:]

    wider(4)

    def p2_copy(xx):
        return pltpu.make_async_remote_copy(
            src_ref=st,
            dst_ref=xbuf.at[x],
            send_sem=p2_send.at[xx],
            recv_sem=p2_recv.at[x],
            device_id=at(xx, z, k),
            device_id_type=MESH,
        )

    def p3_remote(i, kk):
        return pltpu.make_async_remote_copy(
            src_ref=obuf.at[i],
            dst_ref=sbuf.at[z // 2],
            send_sem=p3_send.at[NC * i + kk],
            recv_sem=p3_recv.at[0],
            device_id=at(x, i, kk),
            device_id_type=MESH,
        )

    @pl.when(handler)
    def _():
        pltpu.make_async_copy(hbuf, hbuf, p1_recv.at[0]).wait()
        def join(a, b):
            return a + b - dot2(a, b[:128].astype(BF16))

        twos = []
        for i in range(0, 8, 2):
            a, b = hbuf[i], hbuf[i + 1]
            twos.append(a.astype(F32) + b.astype(F32) - dot(a, b[:128]))
        fours = [join(a, b) for a, b in zip(twos[::2], twos[1::2])]
        row = join(fours[0], fours[1])
        st[...] = row.astype(BF16)
        for xx in range(1, NX):

            @pl.when(x < xx)
            def _():
                p2_copy(xx).start()

        def join_leaf(a, i):
            b = hbuf[i]
            return a + b.astype(F32) - dot2(a, b[:128])

        six = join(fours[0], twos[2])
        ahead = [
            hbuf[0].astype(F32),
            twos[0],
            join_leaf(twos[0], 2),
            fours[0],
            join_leaf(fours[0], 4),
            six,
            join_leaf(six, 6),
        ]
        for i in range(NZ - 1):
            ahead_n[i] = ahead[i][:128].astype(BF16)
            ahead_s[i] = ahead[i][128:]

        @pl.when(x == 0)
        def _():
            sin[...] = jnp.zeros((128, 128), F32)

        for o in range(NX - 1):

            @pl.when(x > o)
            def _():
                pltpu.make_async_copy(xbuf.at[o], xbuf.at[o], p2_recv.at[o]).wait()
                new = xbuf[o, 128:].astype(F32)
                if o > 0:
                    now = sin[...]
                    new = now - dot2(now, xbuf[o, :128]) + new
                sin[...] = new

        s0 = sin[...]
        obuf[0] = s0.astype(BF16)
        for i in range(1, NZ):
            obuf[i] = (s0 - dot2(s0, ahead_n[i - 1]) + ahead_s[i - 1]).astype(BF16)
        for i in range(NZ):
            for kk in range(NC):
                me = (z == i) & (k == kk)

                @pl.when(jnp.logical_not(me))
                def _():
                    p3_remote(i, kk).start()

                @pl.when(me)
                def _():
                    pltpu.make_async_copy(obuf.at[i], sbuf.at[z // 2], p3_recv.at[0]).start()

    @pl.when(k == 1)
    def _():
        for h in range(4):
            moved = dot2_nt(gs[h], pair[0, h])
            gs[h] = gs[h] - moved[:, :128]
            os_[h] = os_[h] + moved[:, 128:]

    for h in range(4):
        col = (h // 2) * GROUP + 512 + (h % 2) * 128
        gate = silu(pj[HALO : HALO + TOK, col : col + 128])
        gz[:, h * 128 : h * 128 + 128] = gain_ref[...] * gate
    wo_copy.wait()

    pltpu.make_async_copy(sbuf, sbuf, p3_recv.at[0]).wait()

    def part(yy):
        rows = pl.ds(pl.multiple_of(64 * yy, 64), 64)
        heads = []
        for h in range(4):
            o = os_[h, rows, :] + dot2_nt(gs[h, rows, :], sbuf[h])
            mean = jnp.mean(o * o, axis=-1, keepdims=True)
            o = o * lax.rsqrt(mean + EPS) * gz[rows, h * 128 : h * 128 + 128]
            heads.append(o.astype(BF16))
        return dot(jnp.concatenate(heads, axis=1), wo[...])

    def rs_copy(way, slot):
        n = 3 * way + slot
        return pltpu.make_async_remote_copy(
            src_ref=rst.at[n],
            dst_ref=rbuf.at[n],
            send_sem=rs_send.at[n],
            recv_sem=rs_recv.at[n],
            device_id=(c, up if way == 0 else down),
            device_id_type=MESH,
        )

    far = part(lax.rem(y + 2, ny)).astype(BF16)
    rst[0] = far[:32]
    rs_copy(0, 0).start()
    rst[3] = far[32:]
    rs_copy(1, 0).start()
    above = part(up)
    rst[1] = above[32:].astype(BF16)
    rs_copy(0, 1).start()
    beneath = part(down)
    rst[4] = beneath[:32].astype(BF16)
    rs_copy(1, 1).start()
    rs_copy(0, 0).wait_recv()
    rst[2] = (above[:32] + rbuf[0].astype(F32)).astype(BF16)
    rs_copy(0, 2).start()
    rs_copy(1, 0).wait_recv()
    rst[5] = (beneath[32:] + rbuf[3].astype(F32)).astype(BF16)
    rs_copy(1, 2).start()
    mine = part(y)
    rs_copy(0, 1).wait_recv()
    rs_copy(1, 1).wait_recv()
    top = mine[:32] + rbuf[4].astype(F32)
    low = mine[32:] + rbuf[1].astype(F32)
    rs_copy(0, 2).wait_recv()
    out_ref[:32] = (top + rbuf[2].astype(F32)).astype(BF16)
    rs_copy(1, 2).wait_recv()
    out_ref[32:] = (low + rbuf[5].astype(F32)).astype(BF16)

    for way in range(2):
        for half in range(2):
            ag_copy(way, half, 0).wait_send()
        ag_copy(way, way, 1).wait_send()
        for slot in range(3):
            rs_copy(way, slot).wait_send()

    @pl.when((y == ny - 1) & (c < nctx - 1))
    def _():
        for yy in range(ny):
            halo_copy(yy).wait_send()

    l0_copy(0).wait_send()
    l0_copy(1).wait_send()

    @pl.when(k == 0)
    def _():
        l0_copy(2).wait_send()
        l0_copy(3).wait_send()

    for j in range(2):

        @pl.when(z != 4 * k + 2 * j)
        def _():
            p1_remote(j).wait_send()

    @pl.when(handler)
    def _():
        for xx in range(1, NX):

            @pl.when(x < xx)
            def _():
                p2_copy(xx).wait_send()

        for i in range(NZ):
            for kk in range(NC):

                @pl.when(jnp.logical_not((z == i) & (k == kk)))
                def _():
                    p3_remote(i, kk).wait_send()


def local(ny, layer_in, in_proj, conv_weight, gate_logits, norm_gain, out_proj):
    rows, width = layer_in.shape
    vmem = pl.BlockSpec(memory_space=pltpu.VMEM)
    hbm = pl.BlockSpec(memory_space=pl.ANY)
    dma = pltpu.SemaphoreType.DMA
    return pl.pallas_call(
        functools.partial(kernel, ny),
        out_shape=jax.ShapeDtypeStruct((rows, width), BF16),
        in_specs=[hbm, hbm, vmem, vmem, vmem, hbm],
        out_specs=vmem,
        scratch_shapes=[
            pltpu.VMEM((HALO + TOK, width), BF16),
            pltpu.VMEM(in_proj.shape, BF16),
            pltpu.VMEM((width, 2 * GROUP), BF16),
            pltpu.VMEM((GROUP, 128), F32),
            pltpu.VMEM((HALO + TOK, 2 * GROUP), F32),
            pltpu.VMEM(out_proj.shape, BF16),
            pltpu.VMEM((2, TOK, 128), F32),
            pltpu.VMEM((2, TOK, 128), F32),
            pltpu.VMEM((4, TOK, TOK), F32),
            pltpu.VMEM((4, TOK, 256), F32),
            pltpu.VMEM((4, TOK, 128), F32),
            pltpu.VMEM((4, TOK, 128), F32),
            pltpu.VMEM((TOK, 512), F32),
            pltpu.VMEM((2, 4, 256, 128), BF16),
            pltpu.VMEM((2, 256, 128), BF16),
            pltpu.VMEM((NZ, 256, 128), BF16),
            pltpu.VMEM((256, 128), BF16),
            pltpu.VMEM((NX, 256, 128), BF16),
            pltpu.VMEM((128, 128), F32),
            pltpu.VMEM((NZ, 128, 128), BF16),
            pltpu.VMEM((4, 128, 128), BF16),
            pltpu.VMEM((NZ - 1, 128, 128), BF16),
            pltpu.VMEM((NZ - 1, 128, 128), F32),
            pltpu.VMEM((6, 32, width), BF16),
            pltpu.VMEM((6, 32, width), BF16),
            pltpu.SemaphoreType.REGULAR((5,)),
            dma((4,)),
            dma((2,)),
            dma((6,)),
            dma((6,)),
            dma((4,)),
            dma((1,)),
            dma((4,)),
            dma((4,)),
            dma((4,)),
            dma((1,)),
            dma((2 * NX,)),
            dma((NX,)),
            dma((NZ * NC,)),
            dma((1,)),
            dma((6,)),
            dma((6,)),
        ],
        compiler_params=pltpu.CompilerParams(
            collective_id=0, has_side_effects=True, vmem_limit_bytes=56 << 20
        ),
    )(layer_in, in_proj, conv_weight, gate_logits, norm_gain.reshape(1, -1), out_proj)


def solution(mesh):
    in_specs = (
        P(("ctx", "head"), None),
        P(None, "head", None),
        P(None, "head", None),
        P(None, "head", "ctx"),
        P(),
        P("head", None),
    )
    out_specs = P(("ctx", "head"), None)
    return jax.shard_map(
        functools.partial(local, mesh.shape["head"]),
        mesh=mesh,
        in_specs=in_specs,
        out_specs=out_specs,
        check_vma=False,
    )
```

```python
import functools

import jax
import jax.numpy as jnp
from jax import lax
from jax.experimental import pallas as pl
from jax.experimental.pallas import tpu as pltpu
from jax.sharding import PartitionSpec as P

NX, NZ, NC = 4, 8, 2
DK = 128
GROUP = 768
TOK = 256
HALO = 16
EPS = 1e-06
MESH = pl.DeviceIdType.MESH
F32, BF16 = jnp.float32, jnp.bfloat16


def dot(a, b):
    return lax.dot_general(a, b, (((1,), (0,)), ((), ())), preferred_element_type=F32)


def dot_nt(a, b):
    return lax.dot_general(a, b, (((1,), (1,)), ((), ())), preferred_element_type=F32)


def split(a):
    hi = a.astype(BF16)
    return hi, (a - hi.astype(F32)).astype(BF16)


def dot3(a, b):
    ah, al = split(a)
    bh, bl = split(b)
    if a.shape[1] != 128:
        return dot(ah, bh) + (dot(al, bh) + dot(ah, bl))
    left = jnp.concatenate([ah, al], axis=1)
    if b.shape[1] != 128:
        return dot(left, jnp.concatenate([bh, bh], axis=0)) + dot(ah, bl)
    upper = jnp.concatenate([bh, bl], axis=1)
    lower = jnp.concatenate([bh, jnp.zeros_like(bh)], axis=1)
    wide = dot(left, jnp.concatenate([upper, lower], axis=0))
    return wide[:, :128] + wide[:, 128:]


def dot3_nt(a, b):
    ah, al = split(a)
    bh, bl = split(b)
    left, right = jnp.concatenate([ah, al], axis=1), jnp.concatenate([bh, bh], axis=1)
    return dot_nt(left, right) + dot_nt(ah, bl)


def dot2(a, b):
    ah, al = split(a)
    return dot(jnp.concatenate([ah, al], axis=1), jnp.concatenate([b, b], axis=0))


def dot2_nt(a, b):
    ah, al = split(a)
    return dot_nt(jnp.concatenate([ah, al], axis=1), jnp.concatenate([b, b], axis=1))


def iota(shape, dim):
    return lax.broadcasted_iota(jnp.int32, shape, dim)


def silu(a):
    return a * jax.nn.sigmoid(a)


def log1p(u):
    series = u * (1.0 - u * (0.5 - u * (1.0 / 3.0 - u * 0.25)))
    return jnp.where(u < 1.0 / 64.0, series, jnp.log(1.0 + u))


def kernel(
    ny,
    x_ref,
    w_ref,
    cw_hbm,
    gate_hbm,
    gain_hbm,
    wo_ref,
    out_ref,
    cw_ref,
    gate_ref,
    gain_ref,
    xg,
    w3,
    w2,
    tmp,
    pj,
    wo,
    qs,
    ks,
    dec,
    wus,
    gs,
    os_,
    gz,
    pair,
    comb,
    hbuf,
    st,
    xbuf,
    sin,
    obuf,
    sbuf,
    ahead_n,
    ahead_s,
    rst,
    rbuf,
    round_sem,
    w_sem,
    loc_sem,
    ag_send,
    ag_recv,
    halo_send,
    halo_recv,
    l0_send,
    l0_recv,
    p1_send,
    p1_recv,
    p2_send,
    p2_recv,
    p3_send,
    p3_recv,
    rs_send,
    rs_recv,
):
    c = lax.axis_index("ctx")
    y = lax.axis_index("head")
    nctx = NX * NZ * NC
    k = lax.rem(c, NC)
    z = lax.rem(c // NC, NZ)
    x = c // (NC * NZ)
    handler = (k == z // (NZ // NC)) & (lax.rem(z, 2) == 0)

    def at(xx, zz, kk):
        return ((xx * NZ + zz) * NC + kk, y)

    xg[0:HALO, :] = jnp.zeros((HALO, xg.shape[1]), BF16)

    rows_w = w3.shape[0] // 4
    w_copies = []
    for i in range(4):
        part = pl.ds(i * rows_w, rows_w)
        w_copies.append(pltpu.make_async_copy(w_ref.at[part], w3.at[part], w_sem.at[i]))
        w_copies[-1].start()
    own_x = pltpu.make_async_copy(x_ref, xg.at[pl.ds(HALO, 64)], loc_sem.at[0])
    gate_copy = pltpu.make_async_copy(gate_hbm, gate_ref, loc_sem.at[2])
    cw_copy = pltpu.make_async_copy(cw_hbm, cw_ref, loc_sem.at[3])
    gain_copy = pltpu.make_async_copy(gain_hbm, gain_ref, loc_sem.at[4])

    barrier = pltpu.get_barrier_semaphore()

    def hello(target):
        pl.semaphore_signal(barrier, inc=1, device_id=target, device_id_type=MESH)

    up, down = lax.rem(y + 1, ny), lax.rem(y + ny - 1, ny)
    hello((c, up))
    hello((c, down))
    hello((lax.rem(c + 1, nctx), y))
    hello((lax.rem(c + nctx - 1, nctx), y))

    @pl.when(c > 0)
    def _():
        hello((c - 1, ny - 1))

    own_x.start()
    gate_copy.start()
    cw_copy.start()
    gain_copy.start()
    halo_out = jnp.where((y == ny - 1) & (c < nctx - 1), ny, 0)
    pl.semaphore_wait(barrier, 4 + halo_out)

    def tell(n):
        for step in (2**n, nctx - 2**n):
            pl.semaphore_signal(
                round_sem.at[n],
                inc=1,
                device_id=(lax.rem(c + step, nctx), y),
                device_id_type=MESH,
            )

    def wider(n):
        pl.semaphore_wait(round_sem.at[n], 2)
        if n < 4:
            tell(n + 1)

    def block_rows(slot, half):
        return pl.ds(HALO + 64 * slot + 32 * half, 32)

    def ag_copy(way, half, hop):
        n = 3 * way + (2 if hop else (half if way == 0 else 1 - half))
        return pltpu.make_async_remote_copy(
            src_ref=xg.at[block_rows(1 + way, half)] if hop else x_ref.at[pl.ds(32 * half, 32)],
            dst_ref=xg.at[block_rows(3 if hop else 1 + way, half)],
            send_sem=ag_send.at[n],
            recv_sem=ag_recv.at[n],
            device_id=(c, up if way == 0 else down),
            device_id_type=MESH,
        )

    def halo_copy(yy):
        return pltpu.make_async_remote_copy(
            src_ref=x_ref.at[pl.ds(64 - 8, 8)],
            dst_ref=xg.at[pl.ds(HALO - 8, 8)],
            send_sem=halo_send.at[yy],
            recv_sem=halo_recv.at[0],
            device_id=(c + 1, yy),
            device_id_type=MESH,
        )

    ag_copy(0, 0, 0).start()
    ag_copy(1, 1, 0).start()
    ag_copy(0, 1, 0).start()
    ag_copy(1, 0, 0).start()

    @pl.when((y == ny - 1) & (c < nctx - 1))
    def _():
        for yy in range(ny):
            halo_copy(yy).start()

    tell(0)
    wo_copy = pltpu.make_async_copy(wo_ref, wo, loc_sem.at[1])
    wo_copy.start()

    w2d = w3.reshape(2 * w3.shape[0], GROUP)
    for i in range(4):
        w_copies[i].wait()

        @pl.loop(i * rows_w // 64, (i + 1) * rows_w // 64)
        def _(s):
            r = pl.ds(pl.multiple_of(s * 64, 64), 64)
            r2 = pl.ds(pl.multiple_of(s * 128, 128), 128)
            for b in range(0, GROUP, 128):
                tmp[b : b + 128, :] = w2d[r2, b : b + 128].astype(F32)
            for g in range(2):
                for b in range(0, GROUP, 128):
                    piece = tmp[pl.ds(b + g, 64, stride=2), :]
                    w2[r, g * GROUP + b : g * GROUP + b + 128] = piece.astype(BF16)

        if i == 3:
            wider(0)
        if i == 1:
            ag_copy(0, 0, 0).wait_recv()
            ag_copy(0, 0, 1).start()
            ag_copy(1, 1, 0).wait_recv()
            ag_copy(1, 1, 1).start()


    gate_copy.wait()
    cw_copy.wait()
    gain_copy.wait()
    alog = gate_ref[0]
    log_decay = -(jnp.maximum(alog, 0.0) + log1p(jnp.exp(-jnp.abs(alog))))
    beta_row = jax.nn.sigmoid(gate_ref[1])
    both = jnp.concatenate([log_decay, beta_row], axis=0)
    upper = (iota((TOK, TOK), 0) <= iota((TOK, TOK), 1)).astype(F32)
    crow = jnp.dot(both, upper, precision=lax.Precision.HIGHEST, preferred_element_type=F32)
    cols = jnp.concatenate([crow[:4], beta_row], axis=0).T

    own_x.wait()
    ag_copy(0, 1, 0).wait_recv()
    ag_copy(1, 0, 0).wait_recv()

    @pl.when(c > 0)
    def _():
        halo_copy(0).wait_recv()

    def project(slot, count, homes):
        start = 0 if slot == 0 else HALO + 64 * slot
        for b in range(0, 2 * GROUP, 512):
            made = dot(xg[start : start + count, :], w2[:, b : b + 512])
            made = made.astype(BF16).astype(F32)
            offset = 0
            for home, rows in homes:
                pj[pl.ds(home, rows), b : b + 512] = made[offset : offset + rows]
                offset += rows

    def home(yy):
        return pl.multiple_of(HALO + 64 * yy, 16)

    project(0, HALO + 192, [(0, HALO), (home(y), 64), (home(down), 64), (home(up), 64)])
    ag_copy(0, 0, 1).wait_recv()
    ag_copy(1, 1, 1).wait_recv()
    project(3, 64, [(home(lax.rem(y + 2, ny)), 64)])

    wider(1)

    def conv(g, b):
        col = g * GROUP + b * 128
        total = None
        for i in range(4):
            w = cw_ref[i, pl.ds(g, 1), b * 128 : b * 128 + 128]
            term = pj[HALO - 3 + i : HALO - 3 + i + TOK, col : col + 128] * w
            total = term if total is None else total + term
        return silu(total)

    def unit(u):
        return u * lax.rsqrt(jnp.sum(u * u, axis=-1, keepdims=True) + EPS)

    below = iota((TOK, TOK), 0) > iota((TOK, TOK), 1)
    on_or_below = iota((TOK, TOK), 0) >= iota((TOK, TOK), 1)
    i128, j128 = iota((128, 128), 0), iota((128, 128), 1)
    eye = (i128 == j128).astype(F32)

    blocks, lows, rhs = [], [], []
    for g in range(2):
        qs[g] = unit(conv(g, 0)) * (DK**-0.5)
        key = unit(conv(g, 1))
        ks[g] = key
        gram = dot3_nt(key, key)
        for r in range(2):
            h = 2 * g + r
            value = conv(g, 2 + r)
            ccol, bcol = cols[:, h : h + 1], cols[:, 4 + h : 5 + h]
            gap = ccol - crow[h : h + 1, :]
            decay = jnp.where(on_or_below, jnp.exp(jnp.where(on_or_below, gap, 0.0)), 0.0)
            dec[h] = decay
            low = jnp.where(below, bcol * gram * decay, 0.0)
            blocks.append(low[:128, :128])
            blocks.append(low[128:, 128:])
            lows.append(low[128:, :128])
            rhs.append(jnp.concatenate([key * (bcol * jnp.exp(ccol)), value * bcol], axis=1))

    wider(2)

    def same(size):
        return (i128 // size) == (j128 // size)

    power = [jnp.where(same(8), -a, 0.0) for a in blocks]
    inv = [eye + a for a in power]
    for _ in range(2):
        power = [dot3(a, a) for a in power]
        inv = [b + dot3(b, a) for a, b in zip(power, inv)]
    for size in (8, 16, 32, 64):
        off = same(2 * size) & jnp.logical_not(same(size))
        mid = [dot3(jnp.where(off, a, 0.0), b) for a, b in zip(blocks, inv)]
        inv = [b - dot3(b, a) for a, b in zip(mid, inv)]

    first = [dot3(inv[2 * h], rhs[h][:128]) for h in range(4)]
    second = [rhs[h][128:] - dot3(lows[h], first[h]) for h in range(4)]
    second = [dot3(inv[2 * h + 1], second[h]) for h in range(4)]
    for h in range(4):
        wu = jnp.concatenate([first[h], second[h]], axis=0)
        wus[h] = wu
        last = crow[h : h + 1, TOK - 1 : TOK]
        k_dec = ks[h // 2] * jnp.exp(last - cols[:, h : h + 1])
        total = dot3(wu.T, k_dec)
        pair[k, h, 0:128, :] = (eye * (1.0 - jnp.exp(last)) + total[:128]).astype(BF16)
        pair[k, h, 128:256, :] = total[128:].astype(BF16)

    wider(3)

    def l0_copy(h):
        return pltpu.make_async_remote_copy(
            src_ref=pair.at[k, h],
            dst_ref=pair.at[k, h],
            send_sem=l0_send.at[h],
            recv_sem=l0_recv.at[h],
            device_id=(c + 1 - 2 * k, y),
            device_id_type=MESH,
        )

    l0_copy(0).start()
    l0_copy(1).start()

    @pl.when(k == 0)
    def _():
        l0_copy(2).start()
        l0_copy(3).start()

    l0_copy(0).wait_recv()
    l0_copy(1).wait_recv()

    @pl.when(k == 1)
    def _():
        l0_copy(2).wait_recv()
        l0_copy(3).wait_recv()

    for j in range(2):
        h = 2 * k + j
        one, two = pair[0, h], pair[1, h]
        new = one.astype(F32) + two.astype(F32) - dot(one, two[:128])
        comb[j] = new.astype(BF16)

    def p1_remote(j):
        return pltpu.make_async_remote_copy(
            src_ref=comb.at[j],
            dst_ref=hbuf.at[z],
            send_sem=p1_send.at[j],
            recv_sem=p1_recv.at[0],
            device_id=at(x, 4 * k + 2 * j, k),
            device_id_type=MESH,
        )

    for j in range(2):

        @pl.when(z != 4 * k + 2 * j)
        def _():
            p1_remote(j).start()

        @pl.when(z == 4 * k + 2 * j)
        def _():
            pltpu.make_async_copy(comb.at[j], hbuf.at[z], p1_recv.at[0]).start()

    for g in range(2):
        qk = dot3_nt(qs[g], ks[g])
        for r in range(2):
            h = 2 * g + r
            both_parts = dot3(qk * dec[h], wus[h])
            gs[h] = qs[g] * jnp.exp(cols[:, h : h + 1]) - both_parts[:, :128]
            os_[h] = both_parts[:, 128:]

    wider(4)

    def p2_copy(xx):
        return pltpu.make_async_remote_copy(
            src_ref=st,
            dst_ref=xbuf.at[x],
            send_sem=p2_send.at[xx],
            recv_sem=p2_recv.at[x],
            device_id=at(xx, z, k),
            device_id_type=MESH,
        )

    def p3_remote(i):
        return pltpu.make_async_remote_copy(
            src_ref=obuf.at[i],
            dst_ref=sbuf.at[z // 2],
            send_sem=p3_send.at[i],
            recv_sem=p3_recv.at[0],
            device_id=at(x, i, k),
            device_id_type=MESH,
        )

    own_heads = sbuf.at[pl.ds(2 * k, 2)]

    def hand_over():
        return pltpu.make_async_remote_copy(
            src_ref=own_heads,
            dst_ref=own_heads,
            send_sem=p3_send.at[NZ],
            recv_sem=p3_recv.at[1],
            device_id=(c + 1 - 2 * k, y),
            device_id_type=MESH,
        )

    @pl.when(handler)
    def _():
        pltpu.make_async_copy(hbuf, hbuf, p1_recv.at[0]).wait()
        def join(a, b):
            return a + b - dot2(a, b[:128].astype(BF16))

        twos = []
        for i in range(0, 8, 2):
            a, b = hbuf[i], hbuf[i + 1]
            twos.append(a.astype(F32) + b.astype(F32) - dot(a, b[:128]))
        fours = [join(a, b) for a, b in zip(twos[::2], twos[1::2])]
        row = join(fours[0], fours[1])
        st[...] = row.astype(BF16)
        for xx in range(1, NX):

            @pl.when(x < xx)
            def _():
                p2_copy(xx).start()

        def join_leaf(a, i):
            b = hbuf[i]
            return a + b.astype(F32) - dot2(a, b[:128])

        six = join(fours[0], twos[2])
        ahead = [
            hbuf[0].astype(F32),
            twos[0],
            join_leaf(twos[0], 2),
            fours[0],
            join_leaf(fours[0], 4),
            six,
            join_leaf(six, 6),
        ]
        for i in range(NZ - 1):
            ahead_n[i] = ahead[i][:128].astype(BF16)
            ahead_s[i] = ahead[i][128:]

        @pl.when(x == 0)
        def _():
            sin[...] = jnp.zeros((128, 128), F32)

        for o in range(NX - 1):

            @pl.when(x > o)
            def _():
                pltpu.make_async_copy(xbuf.at[o], xbuf.at[o], p2_recv.at[o]).wait()
                new = xbuf[o, 128:].astype(F32)
                if o > 0:
                    now = sin[...]
                    new = now - dot2(now, xbuf[o, :128]) + new
                sin[...] = new

        s0 = sin[...]
        obuf[0] = s0.astype(BF16)
        for i in range(1, NZ):
            obuf[i] = (s0 - dot2(s0, ahead_n[i - 1]) + ahead_s[i - 1]).astype(BF16)
        for i in range(NZ):

            @pl.when(z != i)
            def _():
                p3_remote(i).start()

            @pl.when(z == i)
            def _():
                pltpu.make_async_copy(obuf.at[i], sbuf.at[z // 2], p3_recv.at[0]).start()

    @pl.when(k == 1)
    def _():
        for h in range(4):
            moved = dot2_nt(gs[h], pair[0, h])
            gs[h] = gs[h] - moved[:, :128]
            os_[h] = os_[h] + moved[:, 128:]

    for h in range(4):
        col = (h // 2) * GROUP + 512 + (h % 2) * 128
        gate = silu(pj[HALO : HALO + TOK, col : col + 128])
        gz[:, h * 128 : h * 128 + 128] = gain_ref[...] * gate
    wo_copy.wait()

    pltpu.make_async_copy(own_heads, own_heads, p3_recv.at[0]).wait()
    hand_over().start()
    hand_over().wait_recv()

    def part(yy):
        rows = pl.ds(pl.multiple_of(64 * yy, 64), 64)
        heads = []
        for h in range(4):
            o = os_[h, rows, :] + dot2_nt(gs[h, rows, :], sbuf[h])
            mean = jnp.mean(o * o, axis=-1, keepdims=True)
            o = o * lax.rsqrt(mean + EPS) * gz[rows, h * 128 : h * 128 + 128]
            heads.append(o.astype(BF16))
        return dot(jnp.concatenate(heads, axis=1), wo[...])

    def rs_copy(way, slot):
        n = 3 * way + slot
        return pltpu.make_async_remote_copy(
            src_ref=rst.at[n],
            dst_ref=rbuf.at[n],
            send_sem=rs_send.at[n],
            recv_sem=rs_recv.at[n],
            device_id=(c, up if way == 0 else down),
            device_id_type=MESH,
        )

    far = part(lax.rem(y + 2, ny)).astype(BF16)
    rst[0] = far[:32]
    rs_copy(0, 0).start()
    rst[3] = far[32:]
    rs_copy(1, 0).start()
    above = part(up)
    rst[1] = above[32:].astype(BF16)
    rs_copy(0, 1).start()
    beneath = part(down)
    rst[4] = beneath[:32].astype(BF16)
    rs_copy(1, 1).start()
    rs_copy(0, 0).wait_recv()
    rst[2] = (above[:32] + rbuf[0].astype(F32)).astype(BF16)
    rs_copy(0, 2).start()
    rs_copy(1, 0).wait_recv()
    rst[5] = (beneath[32:] + rbuf[3].astype(F32)).astype(BF16)
    rs_copy(1, 2).start()
    mine = part(y)
    rs_copy(0, 1).wait_recv()
    rs_copy(1, 1).wait_recv()
    top = mine[:32] + rbuf[4].astype(F32)
    low = mine[32:] + rbuf[1].astype(F32)
    rs_copy(0, 2).wait_recv()
    out_ref[:32] = (top + rbuf[2].astype(F32)).astype(BF16)
    rs_copy(1, 2).wait_recv()
    out_ref[32:] = (low + rbuf[5].astype(F32)).astype(BF16)

    for way in range(2):
        for half in range(2):
            ag_copy(way, half, 0).wait_send()
        ag_copy(way, way, 1).wait_send()
        for slot in range(3):
            rs_copy(way, slot).wait_send()

    @pl.when((y == ny - 1) & (c < nctx - 1))
    def _():
        for yy in range(ny):
            halo_copy(yy).wait_send()

    l0_copy(0).wait_send()
    l0_copy(1).wait_send()

    @pl.when(k == 0)
    def _():
        l0_copy(2).wait_send()
        l0_copy(3).wait_send()

    for j in range(2):

        @pl.when(z != 4 * k + 2 * j)
        def _():
            p1_remote(j).wait_send()

    @pl.when(handler)
    def _():
        for xx in range(1, NX):

            @pl.when(x < xx)
            def _():
                p2_copy(xx).wait_send()

        for i in range(NZ):

            @pl.when(z != i)
            def _():
                p3_remote(i).wait_send()

    hand_over().wait_send()


def local(ny, layer_in, in_proj, conv_weight, gate_logits, norm_gain, out_proj):
    rows, width = layer_in.shape
    vmem = pl.BlockSpec(memory_space=pltpu.VMEM)
    hbm = pl.BlockSpec(memory_space=pl.ANY)
    dma = pltpu.SemaphoreType.DMA
    return pl.pallas_call(
        functools.partial(kernel, ny),
        out_shape=pltpu.VMEM((rows, width), BF16),
        in_specs=[hbm] * 6,
        out_specs=vmem,
        scratch_shapes=[
            pltpu.VMEM(conv_weight.shape, F32),
            pltpu.VMEM(gate_logits.shape, F32),
            pltpu.VMEM((1, 128), F32),
            pltpu.VMEM((HALO + TOK, width), BF16),
            pltpu.VMEM(in_proj.shape, BF16),
            pltpu.VMEM((width, 2 * GROUP), BF16),
            pltpu.VMEM((GROUP, 128), F32),
            pltpu.VMEM((HALO + TOK, 2 * GROUP), F32),
            pltpu.VMEM(out_proj.shape, BF16),
            pltpu.VMEM((2, TOK, 128), F32),
            pltpu.VMEM((2, TOK, 128), F32),
            pltpu.VMEM((4, TOK, TOK), F32),
            pltpu.VMEM((4, TOK, 256), F32),
            pltpu.VMEM((4, TOK, 128), F32),
            pltpu.VMEM((4, TOK, 128), F32),
            pltpu.VMEM((TOK, 512), F32),
            pltpu.VMEM((2, 4, 256, 128), BF16),
            pltpu.VMEM((2, 256, 128), BF16),
            pltpu.VMEM((NZ, 256, 128), BF16),
            pltpu.VMEM((256, 128), BF16),
            pltpu.VMEM((NX, 256, 128), BF16),
            pltpu.VMEM((128, 128), F32),
            pltpu.VMEM((NZ, 128, 128), BF16),
            pltpu.VMEM((4, 128, 128), BF16),
            pltpu.VMEM((NZ - 1, 128, 128), BF16),
            pltpu.VMEM((NZ - 1, 128, 128), F32),
            pltpu.VMEM((6, 32, width), BF16),
            pltpu.VMEM((6, 32, width), BF16),
            pltpu.SemaphoreType.REGULAR((5,)),
            dma((4,)),
            dma((5,)),
            dma((6,)),
            dma((6,)),
            dma((4,)),
            dma((1,)),
            dma((4,)),
            dma((4,)),
            dma((4,)),
            dma((1,)),
            dma((2 * NX,)),
            dma((NX,)),
            dma((NZ + 1,)),
            dma((2,)),
            dma((6,)),
            dma((6,)),
        ],
        compiler_params=pltpu.CompilerParams(
            collective_id=0, has_side_effects=True, vmem_limit_bytes=56 << 20
        ),
    )(layer_in, in_proj, conv_weight, gate_logits, norm_gain.reshape(1, -1), out_proj)


def solution(mesh):
    in_specs = (
        P(("ctx", "head"), None),
        P(None, "head", None),
        P(None, "head", None),
        P(None, "head", "ctx"),
        P(),
        P("head", None),
    )
    out_specs = P(("ctx", "head"), None)
    return jax.shard_map(
        functools.partial(local, mesh.shape["head"]),
        mesh=mesh,
        in_specs=in_specs,
        out_specs=out_specs,
        check_vma=False,
    )
```

```python
import functools

import jax
import jax.numpy as jnp
from jax import lax
from jax.experimental import pallas as pl
from jax.experimental.pallas import tpu as pltpu
from jax.sharding import PartitionSpec as P

NX, NZ, NC = 4, 8, 2
DK = 128
GROUP = 768
TOK = 256
HALO = 16
EPS = 1e-06
MESH = pl.DeviceIdType.MESH
F32, BF16 = jnp.float32, jnp.bfloat16


def dot(a, b):
    return lax.dot_general(a, b, (((1,), (0,)), ((), ())), preferred_element_type=F32)


def dot_nt(a, b):
    return lax.dot_general(a, b, (((1,), (1,)), ((), ())), preferred_element_type=F32)


def split(a):
    hi = a.astype(BF16)
    return hi, (a - hi.astype(F32)).astype(BF16)


def dot3(a, b):
    ah, al = split(a)
    bh, bl = split(b)
    if a.shape[1] != 128:
        return dot(ah, bh) + (dot(al, bh) + dot(ah, bl))
    left = jnp.concatenate([ah, al], axis=1)
    if b.shape[1] != 128:
        return dot(left, jnp.concatenate([bh, bh], axis=0)) + dot(ah, bl)
    upper = jnp.concatenate([bh, bl], axis=1)
    lower = jnp.concatenate([bh, jnp.zeros_like(bh)], axis=1)
    wide = dot(left, jnp.concatenate([upper, lower], axis=0))
    return wide[:, :128] + wide[:, 128:]


def dot3_nt(a, b):
    ah, al = split(a)
    bh, bl = split(b)
    left, right = jnp.concatenate([ah, al], axis=1), jnp.concatenate([bh, bh], axis=1)
    return dot_nt(left, right) + dot_nt(ah, bl)


def dot2(a, b):
    ah, al = split(a)
    return dot(jnp.concatenate([ah, al], axis=1), jnp.concatenate([b, b], axis=0))


def dot2_nt(a, b):
    ah, al = split(a)
    return dot_nt(jnp.concatenate([ah, al], axis=1), jnp.concatenate([b, b], axis=1))


def iota(shape, dim):
    return lax.broadcasted_iota(jnp.int32, shape, dim)


def silu(a):
    return a * jax.nn.sigmoid(a)


def log1p(u):
    series = u * (1.0 - u * (0.5 - u * (1.0 / 3.0 - u * 0.25)))
    return jnp.where(u < 1.0 / 64.0, series, jnp.log(1.0 + u))


def kernel(
    ny,
    x_ref,
    w_ref,
    cw_hbm,
    gate_hbm,
    gain_hbm,
    wo_ref,
    out_ref,
    cw_ref,
    gate_ref,
    gain_ref,
    xg,
    w3,
    w2,
    tmp,
    pj,
    wo,
    qs,
    ks,
    dec,
    wus,
    gs,
    os_,
    gz,
    pair,
    comb,
    hbuf,
    st,
    xbuf,
    sin,
    obuf,
    sbuf,
    ahead_n,
    ahead_s,
    rst,
    rbuf,
    round_sem,
    w_sem,
    loc_sem,
    ag_send,
    ag_recv,
    halo_send,
    halo_recv,
    l0_send,
    l0_recv,
    p1_send,
    p1_recv,
    p2_send,
    p2_recv,
    p3_send,
    p3_recv,
    rs_send,
    rs_recv,
):
    c = lax.axis_index("ctx")
    y = lax.axis_index("head")
    nctx = NX * NZ * NC
    k = lax.rem(c, NC)
    z = lax.rem(c // NC, NZ)
    x = c // (NC * NZ)
    handler = (k == z // (NZ // NC)) & (lax.rem(z, 2) == 0)

    def at(xx, zz, kk):
        return ((xx * NZ + zz) * NC + kk, y)

    xg[0:HALO, :] = jnp.zeros((HALO, xg.shape[1]), BF16)

    rows_w = w3.shape[0] // 4
    w_copies = []
    for i in range(4):
        part = pl.ds(i * rows_w, rows_w)
        w_copies.append(pltpu.make_async_copy(w_ref.at[part], w3.at[part], w_sem.at[i]))
        w_copies[-1].start()
    own_x = pltpu.make_async_copy(x_ref, xg.at[pl.ds(HALO, 64)], loc_sem.at[0])
    gate_copy = pltpu.make_async_copy(gate_hbm, gate_ref, loc_sem.at[2])
    cw_copy = pltpu.make_async_copy(cw_hbm, cw_ref, loc_sem.at[3])
    gain_copy = pltpu.make_async_copy(gain_hbm, gain_ref, loc_sem.at[4])

    barrier = pltpu.get_barrier_semaphore()

    def hello(target):
        pl.semaphore_signal(barrier, inc=1, device_id=target, device_id_type=MESH)

    up, down = lax.rem(y + 1, ny), lax.rem(y + ny - 1, ny)
    hello((c, up))
    hello((c, down))
    hello((lax.rem(c + 1, nctx), y))
    hello((lax.rem(c + nctx - 1, nctx), y))

    @pl.when(c > 0)
    def _():
        hello((c - 1, ny - 1))

    own_x.start()
    gate_copy.start()
    cw_copy.start()
    gain_copy.start()
    halo_out = jnp.where((y == ny - 1) & (c < nctx - 1), ny, 0)
    pl.semaphore_wait(barrier, 4 + halo_out)

    def tell(n):
        for step in (2**n, nctx - 2**n):
            pl.semaphore_signal(
                round_sem.at[n],
                inc=1,
                device_id=(lax.rem(c + step, nctx), y),
                device_id_type=MESH,
            )

    def wider(n):
        pl.semaphore_wait(round_sem.at[n], 2)
        if n < 4:
            tell(n + 1)

    def block_rows(slot, half):
        return pl.ds(HALO + 64 * slot + 32 * half, 32)

    def ag_copy(way, half, hop):
        n = 3 * way + (2 if hop else (half if way == 0 else 1 - half))
        return pltpu.make_async_remote_copy(
            src_ref=xg.at[block_rows(1 + way, half)] if hop else x_ref.at[pl.ds(32 * half, 32)],
            dst_ref=xg.at[block_rows(3 if hop else 1 + way, half)],
            send_sem=ag_send.at[n],
            recv_sem=ag_recv.at[n],
            device_id=(c, up if way == 0 else down),
            device_id_type=MESH,
        )

    def halo_copy(yy):
        return pltpu.make_async_remote_copy(
            src_ref=x_ref.at[pl.ds(64 - 8, 8)],
            dst_ref=xg.at[pl.ds(HALO - 8, 8)],
            send_sem=halo_send.at[yy],
            recv_sem=halo_recv.at[0],
            device_id=(c + 1, yy),
            device_id_type=MESH,
        )

    ag_copy(0, 0, 0).start()
    ag_copy(1, 1, 0).start()
    ag_copy(0, 1, 0).start()
    ag_copy(1, 0, 0).start()

    @pl.when((y == ny - 1) & (c < nctx - 1))
    def _():
        for yy in range(ny):
            halo_copy(yy).start()

    tell(0)
    wo_copy = pltpu.make_async_copy(wo_ref, wo, loc_sem.at[1])
    wo_copy.start()

    w2d = w3.reshape(2 * w3.shape[0], GROUP)
    for i in range(4):
        w_copies[i].wait()

        @pl.loop(i * rows_w // 64, (i + 1) * rows_w // 64)
        def _(s):
            r = pl.ds(pl.multiple_of(s * 64, 64), 64)
            r2 = pl.ds(pl.multiple_of(s * 128, 128), 128)
            for b in range(0, GROUP, 128):
                tmp[b : b + 128, :] = w2d[r2, b : b + 128].astype(F32)
            for g in range(2):
                for b in range(0, GROUP, 128):
                    piece = tmp[pl.ds(b + g, 64, stride=2), :]
                    w2[r, g * GROUP + b : g * GROUP + b + 128] = piece.astype(BF16)

        if i == 3:
            wider(0)
        if i == 1:
            ag_copy(0, 0, 0).wait_recv()
            ag_copy(0, 0, 1).start()
            ag_copy(1, 1, 0).wait_recv()
            ag_copy(1, 1, 1).start()


    gate_copy.wait()
    cw_copy.wait()
    gain_copy.wait()
    alog = gate_ref[0]
    log_decay = -(jnp.maximum(alog, 0.0) + log1p(jnp.exp(-jnp.abs(alog))))
    beta_row = jax.nn.sigmoid(gate_ref[1])
    both = jnp.concatenate([log_decay, beta_row], axis=0)
    upper = (iota((TOK, TOK), 0) <= iota((TOK, TOK), 1)).astype(F32)
    crow = jnp.dot(both, upper, precision=lax.Precision.HIGHEST, preferred_element_type=F32)
    cols = jnp.concatenate([crow[:4], beta_row], axis=0).T

    own_x.wait()
    ag_copy(0, 1, 0).wait_recv()
    ag_copy(1, 0, 0).wait_recv()

    @pl.when(c > 0)
    def _():
        halo_copy(0).wait_recv()

    def project(slot, count, homes):
        start = 0 if slot == 0 else HALO + 64 * slot
        for b in range(0, 2 * GROUP, 512):
            made = dot(xg[start : start + count, :], w2[:, b : b + 512])
            made = made.astype(BF16).astype(F32)
            offset = 0
            for home, rows in homes:
                pj[pl.ds(home, rows), b : b + 512] = made[offset : offset + rows]
                offset += rows

    def home(yy):
        return pl.multiple_of(HALO + 64 * yy, 16)

    project(0, HALO + 192, [(0, HALO), (home(y), 64), (home(down), 64), (home(up), 64)])
    ag_copy(0, 0, 1).wait_recv()
    ag_copy(1, 1, 1).wait_recv()
    project(3, 64, [(home(lax.rem(y + 2, ny)), 64)])

    wider(1)

    def conv(g, b):
        col = g * GROUP + b * 128
        total = None
        for i in range(4):
            w = cw_ref[i, pl.ds(g, 1), b * 128 : b * 128 + 128]
            term = pj[HALO - 3 + i : HALO - 3 + i + TOK, col : col + 128] * w
            total = term if total is None else total + term
        return silu(total)

    def unit(u):
        return u * lax.rsqrt(jnp.sum(u * u, axis=-1, keepdims=True) + EPS)

    below = iota((TOK, TOK), 0) > iota((TOK, TOK), 1)
    on_or_below = iota((TOK, TOK), 0) >= iota((TOK, TOK), 1)
    i128, j128 = iota((128, 128), 0), iota((128, 128), 1)
    eye = (i128 == j128).astype(F32)

    blocks, lows, rhs = [], [], []
    for g in range(2):
        qs[g] = unit(conv(g, 0)) * (DK**-0.5)
        key = unit(conv(g, 1))
        ks[g] = key
        gram = dot3_nt(key, key)
        for r in range(2):
            h = 2 * g + r
            value = conv(g, 2 + r)
            ccol, bcol = cols[:, h : h + 1], cols[:, 4 + h : 5 + h]
            gap = ccol - crow[h : h + 1, :]
            decay = jnp.where(on_or_below, jnp.exp(jnp.where(on_or_below, gap, 0.0)), 0.0)
            dec[h] = decay
            low = jnp.where(below, bcol * gram * decay, 0.0)
            blocks.append(low[:128, :128])
            blocks.append(low[128:, 128:])
            lows.append(low[128:, :128])
            rhs.append(jnp.concatenate([key * (bcol * jnp.exp(ccol)), value * bcol], axis=1))

    wider(2)

    def same(size):
        return (i128 // size) == (j128 // size)

    power = [jnp.where(same(8), -a, 0.0) for a in blocks]
    inv = [eye + a for a in power]
    for _ in range(2):
        power = [dot3(a, a) for a in power]
        inv = [b + dot3(b, a) for a, b in zip(power, inv)]
    for size in (8, 16, 32, 64):
        off = same(2 * size) & jnp.logical_not(same(size))
        mid = [dot3(jnp.where(off, a, 0.0), b) for a, b in zip(blocks, inv)]
        inv = [b - dot3(b, a) for a, b in zip(mid, inv)]

    first = [dot3(inv[2 * h], rhs[h][:128]) for h in range(4)]
    second = [rhs[h][128:] - dot3(lows[h], first[h]) for h in range(4)]
    second = [dot3(inv[2 * h + 1], second[h]) for h in range(4)]
    for h in range(4):
        wu = jnp.concatenate([first[h], second[h]], axis=0)
        wus[h] = wu
        last = crow[h : h + 1, TOK - 1 : TOK]
        k_dec = ks[h // 2] * jnp.exp(last - cols[:, h : h + 1])
        total = dot3(wu.T, k_dec)
        pair[k, h, 0:128, :] = (eye * (1.0 - jnp.exp(last)) + total[:128]).astype(BF16)
        pair[k, h, 128:256, :] = total[128:].astype(BF16)

    def l0_copy(h):
        return pltpu.make_async_remote_copy(
            src_ref=pair.at[k, h],
            dst_ref=pair.at[k, h],
            send_sem=l0_send.at[h],
            recv_sem=l0_recv.at[h],
            device_id=(c + 1 - 2 * k, y),
            device_id_type=MESH,
        )

    l0_copy(0).start()
    l0_copy(1).start()

    @pl.when(k == 0)
    def _():
        l0_copy(2).start()
        l0_copy(3).start()

    wider(3)
    l0_copy(0).wait_recv()
    l0_copy(1).wait_recv()

    @pl.when(k == 1)
    def _():
        l0_copy(2).wait_recv()
        l0_copy(3).wait_recv()

    def p1_remote(j):
        return pltpu.make_async_remote_copy(
            src_ref=comb.at[j],
            dst_ref=hbuf.at[z],
            send_sem=p1_send.at[j],
            recv_sem=p1_recv.at[0],
            device_id=at(x, 4 * k + 2 * j, k),
            device_id_type=MESH,
        )

    for j in range(2):
        h = 2 * k + j
        one, two = pair[0, h], pair[1, h]
        new = one.astype(F32) + two.astype(F32) - dot(one, two[:128])
        comb[j] = new.astype(BF16)

        @pl.when(z != 4 * k + 2 * j)
        def _():
            p1_remote(j).start()

        @pl.when(z == 4 * k + 2 * j)
        def _():
            pltpu.make_async_copy(comb.at[j], hbuf.at[z], p1_recv.at[0]).start()

    for g in range(2):
        qk = dot3_nt(qs[g], ks[g])
        for r in range(2):
            h = 2 * g + r
            both_parts = dot3(qk * dec[h], wus[h])
            gs[h] = qs[g] * jnp.exp(cols[:, h : h + 1]) - both_parts[:, :128]
            os_[h] = both_parts[:, 128:]

    wider(4)

    def p2_copy(xx):
        return pltpu.make_async_remote_copy(
            src_ref=st,
            dst_ref=xbuf.at[x],
            send_sem=p2_send.at[xx],
            recv_sem=p2_recv.at[x],
            device_id=at(xx, z, k),
            device_id_type=MESH,
        )

    def p3_remote(i):
        return pltpu.make_async_remote_copy(
            src_ref=obuf.at[i],
            dst_ref=sbuf.at[z // 2],
            send_sem=p3_send.at[i],
            recv_sem=p3_recv.at[0],
            device_id=at(x, i, k),
            device_id_type=MESH,
        )

    own_heads = sbuf.at[pl.ds(2 * k, 2)]

    def hand_over():
        return pltpu.make_async_remote_copy(
            src_ref=own_heads,
            dst_ref=own_heads,
            send_sem=p3_send.at[NZ],
            recv_sem=p3_recv.at[1],
            device_id=(c + 1 - 2 * k, y),
            device_id_type=MESH,
        )

    @pl.when(handler)
    def _():
        pltpu.make_async_copy(hbuf, hbuf, p1_recv.at[0]).wait()
        def join(a, b):
            return a + b - dot2(a, b[:128].astype(BF16))

        twos = []
        for i in range(0, 8, 2):
            a, b = hbuf[i], hbuf[i + 1]
            twos.append(a.astype(F32) + b.astype(F32) - dot(a, b[:128]))
        fours = [join(a, b) for a, b in zip(twos[::2], twos[1::2])]
        row = join(fours[0], fours[1])
        st[...] = row.astype(BF16)
        for xx in range(1, NX):

            @pl.when(x < xx)
            def _():
                p2_copy(xx).start()

        def join_leaf(a, i):
            b = hbuf[i]
            return a + b.astype(F32) - dot2(a, b[:128])

        six = join(fours[0], twos[2])
        ahead = [
            hbuf[0].astype(F32),
            twos[0],
            join_leaf(twos[0], 2),
            fours[0],
            join_leaf(fours[0], 4),
            six,
            join_leaf(six, 6),
        ]
        for i in range(NZ - 1):
            ahead_n[i] = ahead[i][:128].astype(BF16)
            ahead_s[i] = ahead[i][128:]

        @pl.when(x == 0)
        def _():
            sin[...] = jnp.zeros((128, 128), F32)

        for o in range(NX - 1):

            @pl.when(x > o)
            def _():
                pltpu.make_async_copy(xbuf.at[o], xbuf.at[o], p2_recv.at[o]).wait()
                new = xbuf[o, 128:].astype(F32)
                if o > 0:
                    now = sin[...]
                    new = now - dot2(now, xbuf[o, :128]) + new
                sin[...] = new

        s0 = sin[...]
        obuf[0] = s0.astype(BF16)
        for i in range(1, NZ):
            obuf[i] = (s0 - dot2(s0, ahead_n[i - 1]) + ahead_s[i - 1]).astype(BF16)
        for i in range(NZ):

            @pl.when(z != i)
            def _():
                p3_remote(i).start()

            @pl.when(z == i)
            def _():
                pltpu.make_async_copy(obuf.at[i], sbuf.at[z // 2], p3_recv.at[0]).start()

    @pl.when(k == 1)
    def _():
        for h in range(4):
            moved = dot2_nt(gs[h], pair[0, h])
            gs[h] = gs[h] - moved[:, :128]
            os_[h] = os_[h] + moved[:, 128:]

    for h in range(4):
        col = (h // 2) * GROUP + 512 + (h % 2) * 128
        gate = silu(pj[HALO : HALO + TOK, col : col + 128])
        gz[:, h * 128 : h * 128 + 128] = gain_ref[...] * gate
    wo_copy.wait()

    pltpu.make_async_copy(own_heads, own_heads, p3_recv.at[0]).wait()
    hand_over().start()
    hand_over().wait_recv()

    def part(yy):
        rows = pl.ds(pl.multiple_of(64 * yy, 64), 64)
        heads = []
        for h in range(4):
            o = os_[h, rows, :] + dot2_nt(gs[h, rows, :], sbuf[h])
            mean = jnp.mean(o * o, axis=-1, keepdims=True)
            o = o * lax.rsqrt(mean + EPS) * gz[rows, h * 128 : h * 128 + 128]
            heads.append(o.astype(BF16))
        return dot(jnp.concatenate(heads, axis=1), wo[...])

    def rs_copy(way, slot):
        n = 3 * way + slot
        return pltpu.make_async_remote_copy(
            src_ref=rst.at[n],
            dst_ref=rbuf.at[n],
            send_sem=rs_send.at[n],
            recv_sem=rs_recv.at[n],
            device_id=(c, up if way == 0 else down),
            device_id_type=MESH,
        )

    far = part(lax.rem(y + 2, ny)).astype(BF16)
    rst[0] = far[:32]
    rs_copy(0, 0).start()
    rst[3] = far[32:]
    rs_copy(1, 0).start()
    above = part(up)
    rst[1] = above[32:].astype(BF16)
    rs_copy(0, 1).start()
    beneath = part(down)
    rst[4] = beneath[:32].astype(BF16)
    rs_copy(1, 1).start()
    rs_copy(0, 0).wait_recv()
    rst[2] = (above[:32] + rbuf[0].astype(F32)).astype(BF16)
    rs_copy(0, 2).start()
    rs_copy(1, 0).wait_recv()
    rst[5] = (beneath[32:] + rbuf[3].astype(F32)).astype(BF16)
    rs_copy(1, 2).start()
    mine = part(y)
    rs_copy(0, 1).wait_recv()
    rs_copy(1, 1).wait_recv()
    top = mine[:32] + rbuf[4].astype(F32)
    low = mine[32:] + rbuf[1].astype(F32)
    rs_copy(0, 2).wait_recv()
    out_ref[:32] = (top + rbuf[2].astype(F32)).astype(BF16)
    rs_copy(1, 2).wait_recv()
    out_ref[32:] = (low + rbuf[5].astype(F32)).astype(BF16)

    for way in range(2):
        for half in range(2):
            ag_copy(way, half, 0).wait_send()
        ag_copy(way, way, 1).wait_send()
        for slot in range(3):
            rs_copy(way, slot).wait_send()

    @pl.when((y == ny - 1) & (c < nctx - 1))
    def _():
        for yy in range(ny):
            halo_copy(yy).wait_send()

    l0_copy(0).wait_send()
    l0_copy(1).wait_send()

    @pl.when(k == 0)
    def _():
        l0_copy(2).wait_send()
        l0_copy(3).wait_send()

    for j in range(2):

        @pl.when(z != 4 * k + 2 * j)
        def _():
            p1_remote(j).wait_send()

    @pl.when(handler)
    def _():
        for xx in range(1, NX):

            @pl.when(x < xx)
            def _():
                p2_copy(xx).wait_send()

        for i in range(NZ):

            @pl.when(z != i)
            def _():
                p3_remote(i).wait_send()

    hand_over().wait_send()


def local(ny, layer_in, in_proj, conv_weight, gate_logits, norm_gain, out_proj):
    rows, width = layer_in.shape
    vmem = pl.BlockSpec(memory_space=pltpu.VMEM)
    hbm = pl.BlockSpec(memory_space=pl.ANY)
    dma = pltpu.SemaphoreType.DMA
    return pl.pallas_call(
        functools.partial(kernel, ny),
        out_shape=pltpu.VMEM((rows, width), BF16),
        in_specs=[hbm] * 6,
        out_specs=vmem,
        scratch_shapes=[
            pltpu.VMEM(conv_weight.shape, F32),
            pltpu.VMEM(gate_logits.shape, F32),
            pltpu.VMEM((1, 128), F32),
            pltpu.VMEM((HALO + TOK, width), BF16),
            pltpu.VMEM(in_proj.shape, BF16),
            pltpu.VMEM((width, 2 * GROUP), BF16),
            pltpu.VMEM((GROUP, 128), F32),
            pltpu.VMEM((HALO + TOK, 2 * GROUP), F32),
            pltpu.VMEM(out_proj.shape, BF16),
            pltpu.VMEM((2, TOK, 128), F32),
            pltpu.VMEM((2, TOK, 128), F32),
            pltpu.VMEM((4, TOK, TOK), F32),
            pltpu.VMEM((4, TOK, 256), F32),
            pltpu.VMEM((4, TOK, 128), F32),
            pltpu.VMEM((4, TOK, 128), F32),
            pltpu.VMEM((TOK, 512), F32),
            pltpu.VMEM((2, 4, 256, 128), BF16),
            pltpu.VMEM((2, 256, 128), BF16),
            pltpu.VMEM((NZ, 256, 128), BF16),
            pltpu.VMEM((256, 128), BF16),
            pltpu.VMEM((NX, 256, 128), BF16),
            pltpu.VMEM((128, 128), F32),
            pltpu.VMEM((NZ, 128, 128), BF16),
            pltpu.VMEM((4, 128, 128), BF16),
            pltpu.VMEM((NZ - 1, 128, 128), BF16),
            pltpu.VMEM((NZ - 1, 128, 128), F32),
            pltpu.VMEM((6, 32, width), BF16),
            pltpu.VMEM((6, 32, width), BF16),
            pltpu.SemaphoreType.REGULAR((5,)),
            dma((4,)),
            dma((5,)),
            dma((6,)),
            dma((6,)),
            dma((4,)),
            dma((1,)),
            dma((4,)),
            dma((4,)),
            dma((4,)),
            dma((1,)),
            dma((2 * NX,)),
            dma((NX,)),
            dma((NZ + 1,)),
            dma((2,)),
            dma((6,)),
            dma((6,)),
        ],
        compiler_params=pltpu.CompilerParams(
            collective_id=0, has_side_effects=True, vmem_limit_bytes=56 << 20
        ),
    )(layer_in, in_proj, conv_weight, gate_logits, norm_gain.reshape(1, -1), out_proj)


def solution(mesh):
    in_specs = (
        P(("ctx", "head"), None),
        P(None, "head", None),
        P(None, "head", None),
        P(None, "head", "ctx"),
        P(),
        P("head", None),
    )
    out_specs = P(("ctx", "head"), None)
    return jax.shard_map(
        functools.partial(local, mesh.shape["head"]),
        mesh=mesh,
        in_specs=in_specs,
        out_specs=out_specs,
        check_vma=False,
    )
```
